128 devices in a mesh: dp: 32 (over z, y, core), col: 4 (over x).
Axes of the slice: x: 4, y: 4, z: 4, core: 2. Of those that a mesh axis runs over, the one named last changes fastest.
Arguments:
- tokens: bfloat16 [32768, 8192], P('dp', 'col'), may hold values from -6 to 6
- out_grad: bfloat16 [32768, 8192], P(('dp', 'col')), may hold values from -24 to 24
- weight: float32 [8192, 8192], P('dp', 'col'), may hold values from -6 to 6
- second: float32 [8192, 8192], P('dp', 'col'), may hold values from 0.0001 to 0.001
- momentum: float32 [8192, 512], P(('dp', 'col')), may hold values from -0.12 to 0.12
- sign_seed: int32 [1], replicated, may hold values from 0 to 999999
- step_number: int32 [1], replicated, may hold values from 1 to 999999
Outputs:
- new_weight: float32 [8192, 8192], P('dp', 'col')
- new_second: float32 [8192, 8192], P('dp', 'col')
- new_momentum: float32 [8192, 512], P(('dp', 'col'))
The draws below stay inside these ranges and needn't reach their ends.
All inputs are finite; a program needn't handle non-finite values.
Results may differ from the reference program's by a relative error of at most 0.00097.
Values may be sent and summed in bfloat16 or wider, within the bound.
A program may use at most 128 MiB of HBM per device.

```python
import math
import jax
import jax.numpy as jnp
from jax import lax

DOUT = 8192
DIN = 8192
RANK = 512
TOKENS = 32768


def strengthened(drawn, key, source, target, parts, factor):
    def block_of(axis_at):
        return (jnp.arange(drawn.shape[axis_at]) // (drawn.shape[axis_at] // parts)).reshape((-1,) + (1,) * (drawn.ndim - 1 - axis_at))

    near = jax.random.permutation(key, parts)[block_of(target)]
    second = (block_of(target) + parts // 2) % parts
    return jnp.where((block_of(source) == near) | (block_of(source) == second), factor * drawn, drawn)


def shard_levels(key, extent, cuts, low, top_value):
    def one(axis_at, shards_of):
        steps = jax.random.uniform(jax.random.fold_in(jax.random.fold_in(key, 6), axis_at), (shards_of,), jnp.float32, low / len(cuts), top_value / len(cuts))
        return jnp.repeat(jnp.exp(steps), extent[axis_at] // shards_of).reshape((-1,) + (1,) * (len(extent) - axis_at - 1))

    factor_of = one(*cuts[0])
    for cut in cuts[1:]:
        factor_of = factor_of * one(*cut)
    return factor_of


def normal_values(own_key, dims, spread, most, cuts=(), dtype=jnp.bfloat16):
    values = jax.random.normal(own_key, dims, jnp.float32) * spread
    if len(cuts) > 0:
        values = shard_levels(own_key, dims, cuts, -0.22, 0.18) * values
    return jnp.clip(values, min=-most, max=most).astype(dtype)


def heavy_noise(key, extent, deviation, reach, split, heavy, dtype=jnp.bfloat16):
    array = deviation * jax.random.normal(key, extent, jnp.float32)
    if split:
        array = array * shard_levels(key, extent, split, -0.22, 0.18)
    return jnp.clip(strengthened(array, jax.random.fold_in(key, 3), *heavy), -reach, reach).astype(dtype)


def setup_inputs(seed: int = 0) -> dict:
    keys = jax.random.split(jax.random.key(seed), 8)
    return {
        "tokens": normal_values(keys[0], (TOKENS, DIN), 1.0, 6.0, ((0, 32), (1, 4))),
        "out_grad": heavy_noise(keys[1], (TOKENS, DOUT), 1.0, 24.0, ((0, 128),), (0, 1, 128, 5.5)),
        "weight": normal_values(keys[2], (DOUT, DIN), 1.0, 6.0, ((0, 32), (1, 4)), jnp.float32),
        "second": jnp.clip(jnp.exp(math.log(0.001) - 2.3025852 * jax.random.uniform(keys[3], (DOUT, DIN), jnp.float32) ** shard_levels(keys[3], (DOUT, DIN), ((0, 32), (1, 4)), -0.2, 0.2)), 0.0001, 0.001),
        "momentum": normal_values(keys[4], (DOUT, RANK), 0.02, 0.12, ((0, 128),), jnp.float32),
        "sign_seed": jax.random.randint(keys[5], (1,), 0, 1000000).astype(jnp.int32),
        "step_number": jax.random.randint(keys[6], (1,), 1, 1000000).astype(jnp.int32),
    }


def sign_table(sign_seed, step_number, first_row, row_count, low_rank):
    row_ids = first_row + lax.iota(jnp.int32, row_count)
    col_ids = lax.iota(jnp.int32, low_rank)
    flat_index = row_ids[:, None] * low_rank + col_ids[None, :]
    hashed = flat_index * 747796405 + sign_seed[0] * 1664525 + step_number[0] * 1013904223
    hashed = hashed ^ hashed >> 16 & 65535
    hashed = hashed * 2127912213
    hashed = hashed ^ hashed >> 13 & 524287
    hashed = hashed * 1103515245
    hashed = hashed ^ hashed >> 16 & 65535
    low_bit = hashed >> 20 & 1
    return (1 - 2 * low_bit).astype(jnp.float32)

def reference(tokens, out_grad, weight, second, momentum, sign_seed, step_number):
    inv_root = 1.0 / jnp.sqrt(jnp.float32(RANK))
    sign_block = sign_table(sign_seed, step_number, 0, DIN, RANK)
    sketch = jnp.dot(tokens.astype(jnp.float32), sign_block, preferred_element_type=jnp.float32) * inv_root
    sketch = sketch.astype(jnp.bfloat16)
    projected = lax.dot_general(out_grad.astype(jnp.float32), sketch.astype(jnp.float32), (((0,), (0,)), ((), ())), preferred_element_type=jnp.float32)
    projected = projected / jnp.float32(TOKENS)
    new_momentum = 0.8 * momentum + 0.2 * projected
    dense_grad = lax.dot_general(new_momentum, sign_block, (((1,), (1,)), ((), ())), precision=lax.Precision.HIGHEST, preferred_element_type=jnp.float32) * inv_root
    new_second = 0.95 * second + 0.05 * dense_grad * dense_grad
    new_weight = weight - 0.5 * dense_grad / (jnp.sqrt(new_second) + 1e-08)
    return (new_weight, new_second, new_momentum)
```

```python
import jax
import jax.numpy as jnp
from jax import lax
from jax.experimental import pallas as pl
from jax.experimental.pallas import tpu as pltpu
from jax.sharding import Mesh
from jax.sharding import PartitionSpec as P

DP = ("z", "y", "c")
DP_COL = ("z", "y", "c", "x")
MESH_ID = pl.DeviceIdType.MESH

RING = 4
RANK = 512
CHUNKS = 4
LANES = 128
TAG = 16
DIN_LOCAL = 2048
QUARTER = 256
TOKENS = 32768
TOP = 16000.0
SLOTS = (2, 1, 3)

INDEX_STEP = 747796405
MIX_ONE = 2127912213
MIX_TWO = 1103515245
HASH_ROWS = 64


def wrapped(value):
    value &= 0xFFFFFFFF
    return value - (1 << 32) if value >= 1 << 31 else value


def ring(axis, step):
    return lax.rem(lax.axis_index(axis) + step, RING)


def coded(values):
    top = jnp.max(jnp.abs(values), axis=(0, 1), keepdims=True)
    exponent = jnp.floor(jnp.log2(jnp.maximum(top, 1e-30)))
    whole = jnp.round(values * (jnp.exp2(-exponent) * TOP)).astype(jnp.int16)
    tag = jnp.broadcast_to(exponent, (TAG, LANES)).astype(jnp.int16)
    return whole, tag


def decoded(ref, rows):
    exponent = ref[rows : rows + TAG, :].astype(jnp.float32)[0:1, :]
    return ref[0:rows, :].astype(jnp.float32) * (jnp.exp2(exponent) * (1.0 / TOP))


def store_coded(ref, rows, values):
    whole, tag = coded(values)
    ref[0:rows, :] = whole
    ref[rows : rows + TAG, :] = tag


def hash_signs(offset, first_row, part, out_ref):
    width = out_ref.shape[2]
    shape = (HASH_ROWS, width)
    base = lax.broadcasted_iota(jnp.int32, shape, 0) * wrapped(RANK * INDEX_STEP)
    base += (lax.broadcasted_iota(jnp.int32, shape, 1) + part * width) * INDEX_STEP

    def body(step, carry):
        row = pl.multiple_of(step * HASH_ROWS, HASH_ROWS)
        mixed = base + (offset + (first_row + row) * wrapped(RANK * INDEX_STEP))
        mixed = mixed ^ lax.shift_right_logical(mixed, jnp.int32(16))
        mixed = mixed * MIX_ONE
        mixed = mixed ^ lax.shift_right_logical(mixed, jnp.int32(13))
        mixed = mixed * wrapped(MIX_TWO << 11)
        out_ref[part, pl.ds(row, HASH_ROWS), :] = jnp.where(mixed < 0, -1.0, 1.0).astype(jnp.bfloat16)
        return carry

    lax.fori_loop(0, out_ref.shape[1] // HASH_ROWS, body, 0)


def reduce_kernel(
    seed_ref, step_ref, tokens_ref, grad_ref, momentum_ref,
    rows_ref, signs_ref,
    tok, sg, s_own, s_send, s_recv, sk, og, og_t,
    p_own, p_send, p_recv, q_own, q_send, q_recv, r_recv, rows,
    tok_sem, og_sem, sg_sem, s_ss, s_rs, sk_ss, sk_rs,
    p_ss, p_rs, q_ss, q_rs, r_ss, r_rs, a_ss, a_rs,
):
    x, y, z, c = (lax.axis_index(name) for name in ("x", "y", "z", "c"))
    other = 1 - c
    first = (("y", "z"), ("z", "y"))

    barrier = pltpu.get_barrier_semaphore()
    for axis in ("x", "y", "z"):
        for step in SLOTS:
            pl.semaphore_signal(barrier, inc=1, device_id={axis: ring(axis, step)}, device_id_type=MESH_ID)
    pl.semaphore_signal(barrier, inc=1, device_id={"c": other}, device_id_type=MESH_ID)

    def remote(src, dst, send_sem, recv_sem, where):
        return pltpu.make_async_remote_copy(
            src_ref=src, dst_ref=dst, send_sem=send_sem, recv_sem=recv_sem, device_id=where, device_id_type=MESH_ID
        )

    tok_copies = {}
    for place, step in enumerate((2, 1, 3, 0)):
        at = pl.ds(pl.multiple_of(ring("x", step) * QUARTER, QUARTER), QUARTER)
        tok_copies[step] = pltpu.make_async_copy(tokens_ref.at[at], tok.at[at], tok_sem.at[place])
        tok_copies[step].start()
    mine = pl.ds(pl.multiple_of(c * QUARTER, QUARTER), QUARTER)
    theirs = pl.ds(pl.multiple_of(other * QUARTER, QUARTER), QUARTER)

    def columns(block, core):
        return pl.ds(pl.multiple_of((block * 2 + core) * 256, 256), 256)

    def start_own(block, carry):
        pltpu.make_async_copy(grad_ref.at[:, columns(block, c)], og.at[block, mine], og_sem.at[0]).start()
        return carry

    lax.fori_loop(0, 16, start_own, 0)

    offset = seed_ref[0] * 1664525 + step_ref[0] * 1013904223
    hash_signs(offset, x * DIN_LOCAL, 0, sg)

    pl.semaphore_wait(barrier, 10)

    def start_swap(block, carry):
        remote(grad_ref.at[:, columns(block, other)], og.at[block, mine], og_sem.at[1], og_sem.at[2], {"c": other}).start()
        return carry

    lax.fori_loop(0, 16, start_swap, 0)

    pending = []

    for pair in range(2):
        if pair:
            hash_signs(offset, x * DIN_LOCAL, 1, sg)
            signs_out = pltpu.make_async_copy(sg, signs_ref, sg_sem)
            signs_out.start()
        for step in (2, 1, 3, 0):
            if not pair:
                tok_copies[step].wait()
            at = pl.ds(pl.multiple_of(ring("x", step) * QUARTER, QUARTER), QUARTER)
            part = jnp.dot(tok[at, :], sg[pair], preferred_element_type=jnp.float32)
            for half in range(2):
                k = pair * 2 + half
                values = part[:, half * LANES : (half + 1) * LANES]
                if step == 0:
                    s_own[k] = values
                else:
                    slot = step - 1
                    store_coded(s_send.at[k, slot], QUARTER, values)
                    copy = remote(
                        s_send.at[k, slot], s_recv.at[k, slot], s_ss.at[k, slot], s_rs.at[k, slot], {"x": ring("x", step)}
                    )
                    copy.start()
                    pending.append(copy)

    pltpu.make_async_copy(og.at[:, mine], og.at[:, mine], og_sem.at[0]).wait()
    swap = remote(og.at[:, mine], og.at[:, theirs], og_sem.at[1], og_sem.at[2], {"c": other})
    swap.wait_recv()

    def turn(block, carry):
        turned = og[block].T
        at_z = block // 4
        at_y = lax.rem(block, 4)
        for peer in range(RING):
            og_t[0, at_y, pl.ds(pl.multiple_of(peer * 128 + at_z * 32, 32), 32), :] = turned[peer * 64 : peer * 64 + 32]
            og_t[1, at_z, pl.ds(pl.multiple_of(peer * 128 + at_y * 32, 32), 32), :] = turned[peer * 64 + 32 : peer * 64 + 64]
        return carry

    lax.fori_loop(0, 16, turn, 0)

    def sketch(k):
        total = s_own[k]
        for slot in range(3):
            pltpu.make_async_copy(s_recv.at[k, slot], s_recv.at[k, slot], s_rs.at[k, slot]).wait()
            total += decoded(s_recv.at[k, slot], QUARTER)
        sk[k, mine, :] = (total * (1.0 / jnp.sqrt(jnp.float32(RANK)))).astype(jnp.bfloat16)
        copy = remote(sk.at[k, mine], sk.at[k, mine], sk_ss.at[k], sk_rs.at[k], {"c": other})
        copy.start()
        pending.append(copy)

    def phase_one(k):
        pltpu.make_async_copy(sk.at[k, theirs], sk.at[k, theirs], sk_rs.at[k]).wait()
        right = sk[k]
        for step in (2, 1, 3, 0):
            for h, (axis, _) in enumerate(first):
                part = jnp.dot(og_t[h, ring(axis, step)], right, preferred_element_type=jnp.float32)
                if step == 0:
                    p_own[k, h] = part
                else:
                    slot = step - 1
                    store_coded(p_send.at[k, h, slot], 512, part)
                    copy = remote(
                        p_send.at[k, h, slot], p_recv.at[k, h, slot], p_ss.at[k, h, slot], p_rs.at[k, h, slot],
                        {axis: ring(axis, step)},
                    )
                    copy.start()
                    pending.append(copy)

    def phase_two(k):
        for h in range(2):
            total = p_own[k, h]
            for slot in range(3):
                pltpu.make_async_copy(p_recv.at[k, h, slot], p_recv.at[k, h, slot], p_rs.at[k, h, slot]).wait()
                total += decoded(p_recv.at[k, h, slot], 512)
            p_own[k, h] = total
            for step in (2, 1, 3, 0):
                values = p_own[k, h, pl.ds(pl.multiple_of(ring("x", step) * 128, 128), 128), :]
                if step == 0:
                    q_own[k, h] = values
                else:
                    slot = step - 1
                    store_coded(q_send.at[k, h, slot], 128, values)
                    copy = remote(
                        q_send.at[k, h, slot], q_recv.at[k, h, slot], q_ss.at[k, h, slot], q_rs.at[k, h, slot],
                        {"x": ring("x", step)},
                    )
                    copy.start()
                    pending.append(copy)

    def phase_three(k):
        for h, (_, axis) in enumerate(first):
            total = q_own[k, h]
            for slot in range(3):
                pltpu.make_async_copy(q_recv.at[k, h, slot], q_recv.at[k, h, slot], q_rs.at[k, h, slot]).wait()
                total += decoded(q_recv.at[k, h, slot], 128)
            q_own[k, h] = total
            for step in SLOTS:
                slot = step - 1
                copy = remote(
                    q_own.at[k, h, pl.ds(pl.multiple_of(ring(axis, step) * 32, 32), 32)],
                    r_recv.at[k, h, slot], r_ss.at[k, h, slot], r_rs.at[k, h, slot], {axis: ring(axis, step)},
                )
                copy.start()
                pending.append(copy)

    def finish(k):
        for h, (_, axis) in enumerate(first):
            total = q_own[k, h, pl.ds(pl.multiple_of(lax.axis_index(axis) * 32, 32), 32), :]
            for slot in range(3):
                pltpu.make_async_copy(r_recv.at[k, h, slot], r_recv.at[k, h, slot], r_rs.at[k, h, slot]).wait()
                total += r_recv[k, h, slot]
            projected = total * (1.0 / TOKENS)
            old = momentum_ref[h * 32 : h * 32 + 32, k * LANES : (k + 1) * LANES]
            rows[k, pl.ds(pl.multiple_of(x * 64 + h * 32, 32), 32), :] = 0.8 * old + 0.2 * projected
        at = pl.ds(pl.multiple_of(x * 64, 64), 64)
        for step in SLOTS:
            slot = step - 1
            copy = remote(rows.at[k, at], rows.at[k, at], a_ss.at[k, slot], a_rs.at[k, slot], {"x": ring("x", step)})
            copy.start()
            pending.append(copy)

    for k in range(CHUNKS):
        sketch(k)
        phase_one(k)
    phase_two(0)
    phase_three(0)
    phase_two(1)
    finish(0)
    phase_three(1)
    phase_two(2)
    finish(1)
    phase_three(2)
    phase_two(3)
    finish(2)
    phase_three(3)
    finish(3)

    for k in range(CHUNKS):
        for step in SLOTS:
            at = pl.ds(pl.multiple_of(ring("x", RING - step) * 64, 64), 64)
            pltpu.make_async_copy(rows.at[k, at], rows.at[k, at], a_rs.at[k, step - 1]).wait()
        rows_ref[k] = rows[k]
    swap.wait_send()
    signs_out.wait()
    for copy in pending:
        copy.wait_send()


def reduced(sign_seed, step_number, tokens, out_grad, momentum):
    f32, bf16, i16 = jnp.float32, jnp.bfloat16, jnp.int16
    dma = pltpu.SemaphoreType.DMA
    smem = pl.BlockSpec(memory_space=pltpu.SMEM)
    anywhere = pl.BlockSpec(memory_space=pl.ANY)
    vmem = pl.BlockSpec(memory_space=pltpu.VMEM)
    return pl.pallas_call(
        reduce_kernel,
        out_shape=(
            jax.ShapeDtypeStruct((CHUNKS, 256, LANES), f32),
            jax.ShapeDtypeStruct((2, DIN_LOCAL, 256), bf16),
        ),
        in_specs=[smem, smem, anywhere, anywhere, vmem],
        out_specs=(vmem, anywhere),
        scratch_shapes=[
            pltpu.VMEM((1024, DIN_LOCAL), bf16),
            pltpu.VMEM((2, DIN_LOCAL, 256), bf16),
            pltpu.VMEM((CHUNKS, QUARTER, LANES), f32),
            pltpu.VMEM((CHUNKS, 3, QUARTER + TAG, LANES), i16),
            pltpu.VMEM((CHUNKS, 3, QUARTER + TAG, LANES), i16),
            pltpu.VMEM((CHUNKS, 512, LANES), bf16),
            pltpu.VMEM((16, 512, 256), bf16),
            pltpu.VMEM((2, RING, 512, 512), bf16),
            pltpu.VMEM((CHUNKS, 2, 512, LANES), f32),
            pltpu.VMEM((CHUNKS, 2, 3, 512 + TAG, LANES), i16),
            pltpu.VMEM((CHUNKS, 2, 3, 512 + TAG, LANES), i16),
            pltpu.VMEM((CHUNKS, 2, 128, LANES), f32),
            pltpu.VMEM((CHUNKS, 2, 3, 128 + TAG, LANES), i16),
            pltpu.VMEM((CHUNKS, 2, 3, 128 + TAG, LANES), i16),
            pltpu.VMEM((CHUNKS, 2, 3, 32, LANES), f32),
            pltpu.VMEM((CHUNKS, 256, LANES), f32),
            dma((4,)), dma((3,)), dma,
            dma((CHUNKS, 3)), dma((CHUNKS, 3)), dma((CHUNKS,)), dma((CHUNKS,)),
            dma((CHUNKS, 2, 3)), dma((CHUNKS, 2, 3)),
            dma((CHUNKS, 2, 3)), dma((CHUNKS, 2, 3)),
            dma((CHUNKS, 2, 3)), dma((CHUNKS, 2, 3)),
            dma((CHUNKS, 3)), dma((CHUNKS, 3)),
        ],
        compiler_params=pltpu.CompilerParams(
            collective_id=0, has_side_effects=True, vmem_limit_bytes=48 * 1024 * 1024
        ),
        name="sketch_and_reduce",
    )(sign_seed, step_number, tokens, out_grad, momentum)


COLUMNS = 512


def update_kernel(rows_ref, signs_ref, weight_ref, second_ref, new_weight_ref, new_second_ref, momentum_ref, high, low):
    @pl.when(pl.program_id(0) == 0)
    def _():
        mine = pl.ds(pl.multiple_of(lax.axis_index("x") * 64, 64), 64)
        for k in range(CHUNKS):
            values = rows_ref[k]
            top = values.astype(jnp.bfloat16)
            high[:, k * LANES : (k + 1) * LANES] = top
            low[:, k * LANES : (k + 1) * LANES] = (values - top.astype(jnp.float32)).astype(jnp.bfloat16)
            momentum_ref[:, k * LANES : (k + 1) * LANES] = rows_ref[k, mine, :]

    grad = jnp.zeros((256, COLUMNS), jnp.float32)
    for part in range(2):
        at = slice(part * 256, (part + 1) * 256)
        for left in (high, low):
            grad += lax.dot_general(
                left[:, at], signs_ref[part], (((1,), (1,)), ((), ())), preferred_element_type=jnp.float32
            )
    grad = grad * (1.0 / jnp.sqrt(jnp.float32(RANK)))
    second = 0.95 * second_ref[...] + 0.05 * grad * grad
    new_second_ref[...] = second
    new_weight_ref[...] = weight_ref[...] - 0.5 * grad / (jnp.sqrt(second) + 1e-08)


def updated(rows, signs, weight, second):
    f32 = jnp.float32
    tile = pl.BlockSpec((256, COLUMNS), lambda j: (0, j))
    return pl.pallas_call(
        update_kernel,
        grid=(DIN_LOCAL // COLUMNS,),
        out_shape=(
            jax.ShapeDtypeStruct(weight.shape, f32),
            jax.ShapeDtypeStruct(second.shape, f32),
            jax.ShapeDtypeStruct((64, RANK), f32),
        ),
        in_specs=[
            pl.BlockSpec((CHUNKS, 256, LANES), lambda j: (0, 0, 0)),
            pl.BlockSpec((2, COLUMNS, 256), lambda j: (0, j, 0)),
            tile,
            tile,
        ],
        out_specs=(tile, tile, pl.BlockSpec((64, RANK), lambda j: (0, 0))),
        scratch_shapes=[pltpu.VMEM((256, RANK), jnp.bfloat16), pltpu.VMEM((256, RANK), jnp.bfloat16)],
        compiler_params=pltpu.CompilerParams(vmem_limit_bytes=32 * 1024 * 1024),
        name="dense_update",
    )(rows, signs, weight, second)


def per_device(tokens, out_grad, weight, second, momentum, sign_seed, step_number):
    rows, signs = reduced(sign_seed, step_number, tokens, out_grad, momentum)
    return updated(rows, signs, weight, second)


def solution(mesh):
    torus = Mesh(mesh.devices.reshape(4, 4, 2, mesh.shape["col"]), ("z", "y", "c", "x"))
    return jax.shard_map(
        per_device,
        mesh=torus,
        in_specs=(
            P(DP, "x"),
            P(DP_COL, None),
            P(DP, "x"),
            P(DP, "x"),
            P(DP_COL, None),
            P(),
            P(),
        ),
        out_specs=(P(DP, "x"), P(DP, "x"), P(DP_COL, None)),
        check_vma=False,
    )
```

```python
import jax
import jax.numpy as jnp
from jax import lax
from jax.experimental import pallas as pl
from jax.experimental.pallas import tpu as pltpu
from jax.sharding import Mesh
from jax.sharding import PartitionSpec as P

DP = ("z", "y", "c")
DP_COL = ("z", "y", "c", "x")
MESH_ID = pl.DeviceIdType.MESH

RING = 4
RANK = 512
CHUNKS = 4
LANES = 128
TAG = 16
DIN_LOCAL = 2048
QUARTER = 256
TOKENS = 32768
TOP = 16000.0
SLOTS = (2, 1, 3)

INDEX_STEP = 747796405
MIX_ONE = 2127912213
MIX_TWO = 1103515245
HASH_ROWS = 64


PLAN = (
    ("partial_sketch", 0),
    ("partial_sketch", 1),
    ("sketch", 0),
    ("turn", 0),
    ("phase_one", 0),
    ("sketch", 1),
    ("phase_one", 1),
    ("sketch", 2),
    ("relay", 0),
    ("phase_one", 2),
    ("sketch", 3),
    ("relay", 1),
    ("phase_one", 3),
    ("relay", 2),
    ("phase_two", 0),
    ("relay", 3),
    ("phase_two", 1),
    ("phase_three", 0),
    ("phase_two", 2),
    ("phase_three", 1),
    ("phase_two", 3),
    ("phase_three", 2),
    ("finish", 0),
    ("finish", 1),
    ("phase_three", 3),
    ("finish", 2),
    ("finish", 3),
)


def wrapped(value):
    value &= 0xFFFFFFFF
    return value - (1 << 32) if value >= 1 << 31 else value


def ring(axis, step):
    return lax.rem(lax.axis_index(axis) + step, RING)


def coded(values):
    top = jnp.max(jnp.abs(values), axis=(0, 1), keepdims=True)
    exponent = jnp.floor(jnp.log2(jnp.maximum(top, 1e-30)))
    whole = jnp.round(values * (jnp.exp2(-exponent) * TOP)).astype(jnp.int16)
    tag = jnp.broadcast_to(exponent, (TAG, LANES)).astype(jnp.int16)
    return whole, tag


def decoded(ref, rows):
    exponent = ref[rows : rows + TAG, :].astype(jnp.float32)[0:1, :]
    return ref[0:rows, :].astype(jnp.float32) * (jnp.exp2(exponent) * (1.0 / TOP))


def store_coded(ref, rows, values):
    whole, tag = coded(values)
    ref[0:rows, :] = whole
    ref[rows : rows + TAG, :] = tag


def hash_signs(offset, first_row, part, out_ref):
    width = out_ref.shape[2]
    shape = (HASH_ROWS, width)
    base = lax.broadcasted_iota(jnp.int32, shape, 0) * wrapped(RANK * INDEX_STEP)
    base += (lax.broadcasted_iota(jnp.int32, shape, 1) + part * width) * INDEX_STEP

    def body(step, carry):
        row = pl.multiple_of(step * HASH_ROWS, HASH_ROWS)
        mixed = base + (offset + (first_row + row) * wrapped(RANK * INDEX_STEP))
        mixed = mixed ^ lax.shift_right_logical(mixed, jnp.int32(16))
        mixed = mixed * MIX_ONE
        mixed = mixed ^ lax.shift_right_logical(mixed, jnp.int32(13))
        mixed = mixed * wrapped(MIX_TWO << 11)
        out_ref[part, pl.ds(row, HASH_ROWS), :] = jnp.where(mixed < 0, -1.0, 1.0).astype(jnp.bfloat16)
        return carry

    lax.fori_loop(0, out_ref.shape[1] // HASH_ROWS, body, 0)


def reduce_kernel(
    seed_ref, step_ref, tokens_ref, grad_ref, momentum_ref,
    rows_ref, signs_ref,
    old, tok, sg, s_own, s_send, s_recv, sk, og, og_t,
    p_own, p_send, p_recv, q_own, q_send, q_recv, u_send, u_recv, t_send, t_recv,
    old_sem, tok_sem, og_sem, sg_sem, s_ss, s_rs, sk_ss, sk_rs,
    u_ss, u_rs, p_ss, p_rs, q_ss, q_rs, t_ss, t_rs,
):
    x, y, z, c = (lax.axis_index(name) for name in ("x", "y", "z", "c"))
    other = 1 - c
    first = (("y", "z"), ("z", "y"))

    barrier = pltpu.get_barrier_semaphore()
    for axis in ("x", "y", "z"):
        for step in SLOTS:
            pl.semaphore_signal(barrier, inc=1, device_id={axis: ring(axis, step)}, device_id_type=MESH_ID)
    pl.semaphore_signal(barrier, inc=1, device_id={"c": other}, device_id_type=MESH_ID)

    sems = {
        "s": (s_ss, s_rs), "k": (sk_ss, sk_rs), "u": (u_ss, u_rs), "p": (p_ss, p_rs), "q": (q_ss, q_rs), "t": (t_ss, t_rs)
    }
    sent = {}
    unsent = []

    def remote(src, dst, send_sem, recv_sem, where):
        return pltpu.make_async_remote_copy(
            src_ref=src, dst_ref=dst, send_sem=send_sem, recv_sem=recv_sem, device_id=where, device_id_type=MESH_ID
        )

    def send(kind, at, src, dst, where):
        out, into = sems[kind]
        copy = remote(src, dst, out.at[at], into.at[at], where)
        copy.start()
        sent[kind, at] = copy
        unsent.append((kind, at))

    def left(kind, at):
        sent[kind, at].wait_send()
        unsent.remove((kind, at))

    def arrived(kind, at, ref):
        pltpu.make_async_copy(ref, ref, sems[kind][1].at[at]).wait()

    tok_copies = {}
    for place, step in enumerate((2, 1, 3, 0)):
        at = pl.ds(pl.multiple_of(ring("x", step) * QUARTER, QUARTER), QUARTER)
        tok_copies[step] = pltpu.make_async_copy(tokens_ref.at[at], tok.at[at], tok_sem.at[place])
        tok_copies[step].start()
    mine = pl.ds(pl.multiple_of(c * QUARTER, QUARTER), QUARTER)
    theirs = pl.ds(pl.multiple_of(other * QUARTER, QUARTER), QUARTER)

    def columns(block, core):
        return pl.ds(pl.multiple_of((block * 2 + core) * 256, 256), 256)

    def start_own(block, carry):
        pltpu.make_async_copy(grad_ref.at[:, columns(block, c)], og.at[block, mine], og_sem.at[0]).start()
        return carry

    lax.fori_loop(0, 16, start_own, 0)
    old_copy = pltpu.make_async_copy(momentum_ref, old, old_sem)
    old_copy.start()

    offset = seed_ref[0] * 1664525 + step_ref[0] * 1013904223
    hash_signs(offset, x * DIN_LOCAL, 0, sg)

    pl.semaphore_wait(barrier, 10)

    def start_swap(block, carry):
        remote(grad_ref.at[:, columns(block, other)], og.at[block, mine], og_sem.at[1], og_sem.at[2], {"c": other}).start()
        return carry

    lax.fori_loop(0, 16, start_swap, 0)

    def partial_sketch(pair):
        def send_coded(k, step, values):
            slot = step - 1
            store_coded(s_send.at[k, slot], QUARTER, values)
            send("s", (k, slot), s_send.at[k, slot], s_recv.at[k, slot], {"x": ring("x", step)})

        if pair:
            hash_signs(offset, x * DIN_LOCAL, 1, sg)
            signs_out.start()
        for step in (2, 1, 3, 0):
            if not pair:
                tok_copies[step].wait()
            at = pl.ds(pl.multiple_of(ring("x", step) * QUARTER, QUARTER), QUARTER)
            part = jnp.dot(tok[at, :], sg[pair], preferred_element_type=jnp.float32)
            s_own[2 * pair + 1, step] = part[:, LANES:]
            if step:
                send_coded(2 * pair, step, part[:, :LANES])
            else:
                s_own[2 * pair, step] = part[:, :LANES]
        for step in SLOTS:
            send_coded(2 * pair + 1, step, s_own[2 * pair + 1, step])

    def turn(_):
        pltpu.make_async_copy(og.at[:, mine], og.at[:, mine], og_sem.at[0]).wait()
        swap.wait_recv()

        def body(block, carry):
            turned = og[block].T
            at_z = block // 4
            at_y = lax.rem(block, 4)
            for peer in range(RING):
                row = peer * 64
                og_t[0, at_y, pl.ds(pl.multiple_of(peer * 128 + at_z * 32, 32), 32), :] = turned[row : row + 32]
                og_t[1, at_z, pl.ds(pl.multiple_of(peer * 128 + at_y * 32, 32), 32), :] = turned[row + 32 : row + 64]
            return carry

        lax.fori_loop(0, 16, body, 0)

    def sketch(k):
        total = s_own[k, 0]
        for slot in range(3):
            arrived("s", (k, slot), s_recv.at[k, slot])
            total += decoded(s_recv.at[k, slot], QUARTER)
        sk[k, mine, :] = (total * (1.0 / jnp.sqrt(jnp.float32(RANK)))).astype(jnp.bfloat16)
        send("k", (k,), sk.at[k, mine], sk.at[k, mine], {"c": other})

    def phase_one(k):
        arrived("k", (k,), sk.at[k, theirs])
        right = sk[k]
        for step in (2, 1, 3, 0):
            for h, (axis, _) in enumerate(first):
                part = jnp.dot(og_t[h, ring(axis, step)], right, preferred_element_type=jnp.float32)
                if step == 2:
                    for side, near in enumerate((1, 3)):
                        ref = u_send.at[k, h, side]
                        store_coded(ref, 256, part[side * 256 : side * 256 + 256])
                        send("u", (k, h, side), ref, u_recv.at[k, h, side], {axis: ring(axis, near)})
                else:
                    p_own[k, h, (0, 1, None, 2)[step]] = part

    def relay(k):
        for side, near in enumerate((1, 3)):
            for h, (axis, _) in enumerate(first):
                arrived("u", (k, h, side), u_recv.at[k, h, side])
                rows_at = slice(side * 256, side * 256 + 256)
                p_own[k, h, side + 1, rows_at] += decoded(u_recv.at[k, h, side], 256)
                store_coded(p_send.at[k, h, side], 512, p_own[k, h, side + 1])
                send("p", (k, h, side), p_send.at[k, h, side], p_recv.at[k, h, side], {axis: ring(axis, near)})

    def phase_two(k):
        for h, (_, axis) in enumerate(first):
            total = p_own[k, h, 0]
            for side in range(2):
                arrived("p", (k, h, side), p_recv.at[k, h, side])
                total += decoded(p_recv.at[k, h, side], 512)
            p_own[k, h, 0] = total
            for step in (2, 1, 3, 0):
                at = [pl.ds(pl.multiple_of(peer * 128 + ring(axis, step) * 32, 32), 32) for peer in range(RING)]
                values = jnp.concatenate([p_own[k, h, 0, rows_at, :] for rows_at in at], axis=0)
                if step == 0:
                    q_own[k, h * 128 : h * 128 + 128] = values
                else:
                    slot = step - 1
                    store_coded(q_send.at[k, h, slot], 128, values)
                    send("q", (k, h, slot), q_send.at[k, h, slot], q_recv.at[k, h, slot], {axis: ring(axis, step)})

    def phase_three(k):
        if k == 0:
            old_copy.wait()
        for h in range(2):
            total = q_own[k, h * 128 : h * 128 + 128]
            for slot in range(3):
                arrived("q", (k, h, slot), q_recv.at[k, h, slot])
                total += decoded(q_recv.at[k, h, slot], 128)
            q_own[k, h * 128 : h * 128 + 128] = total * (0.2 / TOKENS)
            at = pl.ds(pl.multiple_of(h * 128 + x * 32, 32), 32)
            q_own[k, at, :] += 0.8 * old[h * 32 : h * 32 + 32, k * LANES : (k + 1) * LANES]
        store_coded(t_send.at[k], 256, q_own[k])
        for step in SLOTS:
            send("t", (k, step - 1), t_send.at[k], t_recv.at[k, step - 1], {"x": ring("x", step)})

    def finish(k):
        total = q_own[k]
        for step in SLOTS:
            arrived("t", (k, step - 1), t_recv.at[k, step - 1])
            total += decoded(t_recv.at[k, step - 1], 256)
        for peer in range(RING):
            for h in range(2):
                row = h * 128 + peer * 32
                rows_ref[k, peer * 64 + h * 32 : peer * 64 + h * 32 + 32, :] = total[row : row + 32]

    signs_out = pltpu.make_async_copy(sg, signs_ref, sg_sem)
    swap = remote(og.at[:, mine], og.at[:, theirs], og_sem.at[1], og_sem.at[2], {"c": other})
    steps = {
        "partial_sketch": partial_sketch, "turn": turn, "sketch": sketch, "phase_one": phase_one, "relay": relay,
        "phase_two": phase_two, "phase_three": phase_three, "finish": finish,
    }
    for name, k in PLAN:
        steps[name](k)
    swap.wait_send()
    signs_out.wait()
    for kind, at in tuple(unsent):
        left(kind, at)


def reduced(sign_seed, step_number, tokens, out_grad, momentum):
    f32, bf16, i16 = jnp.float32, jnp.bfloat16, jnp.int16
    dma = pltpu.SemaphoreType.DMA
    smem = pl.BlockSpec(memory_space=pltpu.SMEM)
    anywhere = pl.BlockSpec(memory_space=pltpu.HBM)
    vmem = pl.BlockSpec(memory_space=pltpu.VMEM)
    return pl.pallas_call(
        reduce_kernel,
        out_shape=(
            jax.ShapeDtypeStruct((CHUNKS, 256, LANES), f32),
            jax.ShapeDtypeStruct((2, DIN_LOCAL, 256), bf16),
        ),
        in_specs=[smem, smem, anywhere, anywhere, anywhere],
        out_specs=(vmem, anywhere),
        scratch_shapes=[
            pltpu.VMEM((64, RANK), f32),
            pltpu.VMEM((1024, DIN_LOCAL), bf16),
            pltpu.VMEM((2, DIN_LOCAL, 256), bf16),
            pltpu.VMEM((CHUNKS, RING, QUARTER, LANES), f32),
            pltpu.VMEM((CHUNKS, 3, QUARTER + TAG, LANES), i16),
            pltpu.VMEM((CHUNKS, 3, QUARTER + TAG, LANES), i16),
            pltpu.VMEM((CHUNKS, 512, LANES), bf16),
            pltpu.VMEM((16, 512, 256), bf16),
            pltpu.VMEM((2, RING, 512, 512), bf16),
            pltpu.VMEM((CHUNKS, 2, 3, 512, LANES), f32),
            pltpu.VMEM((CHUNKS, 2, 2, 512 + TAG, LANES), i16),
            pltpu.VMEM((CHUNKS, 2, 2, 512 + TAG, LANES), i16),
            pltpu.VMEM((CHUNKS, 256, LANES), f32),
            pltpu.VMEM((CHUNKS, 2, 3, 128 + TAG, LANES), i16),
            pltpu.VMEM((CHUNKS, 2, 3, 128 + TAG, LANES), i16),
            pltpu.VMEM((CHUNKS, 2, 2, 256 + TAG, LANES), i16),
            pltpu.VMEM((CHUNKS, 2, 2, 256 + TAG, LANES), i16),
            pltpu.VMEM((CHUNKS, 256 + TAG, LANES), i16),
            pltpu.VMEM((CHUNKS, 3, 256 + TAG, LANES), i16),
            dma, dma((4,)), dma((3,)), dma,
            dma((CHUNKS, 3)), dma((CHUNKS, 3)), dma((CHUNKS,)), dma((CHUNKS,)),
            dma((CHUNKS, 2, 2)), dma((CHUNKS, 2, 2)),
            dma((CHUNKS, 2, 2)), dma((CHUNKS, 2, 2)),
            dma((CHUNKS, 2, 3)), dma((CHUNKS, 2, 3)),
            dma((CHUNKS, 3)), dma((CHUNKS, 3)),
        ],
        compiler_params=pltpu.CompilerParams(
            collective_id=0, has_side_effects=True, vmem_limit_bytes=48 * 1024 * 1024
        ),
        name="sketch_and_reduce",
    )(sign_seed, step_number, tokens, out_grad, momentum)


COLUMNS = 512


def update_kernel(rows_ref, signs_ref, weight_ref, second_ref, new_weight_ref, new_second_ref, momentum_ref, high, low):
    @pl.when(pl.program_id(0) == 0)
    def _():
        mine = pl.ds(pl.multiple_of(lax.axis_index("x") * 64, 64), 64)
        for k in range(CHUNKS):
            values = rows_ref[k]
            top = values.astype(jnp.bfloat16)
            high[:, k * LANES : (k + 1) * LANES] = top
            low[:, k * LANES : (k + 1) * LANES] = (values - top.astype(jnp.float32)).astype(jnp.bfloat16)
            momentum_ref[:, k * LANES : (k + 1) * LANES] = rows_ref[k, mine, :]

    grad = jnp.zeros((256, COLUMNS), jnp.float32)
    for part in range(2):
        at = slice(part * 256, (part + 1) * 256)
        for left in (high, low):
            grad += lax.dot_general(
                left[:, at], signs_ref[part], (((1,), (1,)), ((), ())), preferred_element_type=jnp.float32
            )
    grad = grad * (1.0 / jnp.sqrt(jnp.float32(RANK)))
    second = 0.95 * second_ref[...] + 0.05 * grad * grad
    new_second_ref[...] = second
    new_weight_ref[...] = weight_ref[...] - 0.5 * grad / (jnp.sqrt(second) + 1e-08)


def updated(rows, signs, weight, second):
    f32 = jnp.float32
    tile = pl.BlockSpec((256, COLUMNS), lambda j: (0, j))
    return pl.pallas_call(
        update_kernel,
        grid=(DIN_LOCAL // COLUMNS,),
        out_shape=(
            jax.ShapeDtypeStruct(weight.shape, f32),
            jax.ShapeDtypeStruct(second.shape, f32),
            jax.ShapeDtypeStruct((64, RANK), f32),
        ),
        in_specs=[
            pl.BlockSpec((CHUNKS, 256, LANES), lambda j: (0, 0, 0)),
            pl.BlockSpec((2, COLUMNS, 256), lambda j: (0, j, 0)),
            tile,
            tile,
        ],
        out_specs=(tile, tile, pl.BlockSpec((64, RANK), lambda j: (0, 0))),
        scratch_shapes=[pltpu.VMEM((256, RANK), jnp.bfloat16), pltpu.VMEM((256, RANK), jnp.bfloat16)],
        compiler_params=pltpu.CompilerParams(vmem_limit_bytes=32 * 1024 * 1024),
        name="dense_update",
    )(rows, signs, weight, second)


def per_device(tokens, out_grad, weight, second, momentum, sign_seed, step_number):
    rows, signs = reduced(sign_seed, step_number, tokens, out_grad, momentum)
    return updated(rows, signs, weight, second)


def solution(mesh):
    torus = Mesh(mesh.devices.reshape(4, 4, 2, mesh.shape["col"]), ("z", "y", "c", "x"))
    return jax.shard_map(
        per_device,
        mesh=torus,
        in_specs=(
            P(DP, "x"),
            P(DP_COL, None),
            P(DP, "x"),
            P(DP, "x"),
            P(DP_COL, None),
            P(),
            P(),
        ),
        out_specs=(P(DP, "x"), P(DP, "x"), P(DP_COL, None)),
        check_vma=False,
    )
```

```python
import jax
import jax.numpy as jnp
from jax import lax
from jax.experimental import pallas as pl
from jax.experimental.pallas import tpu as pltpu
from jax.sharding import Mesh
from jax.sharding import PartitionSpec as P

DP = ("z", "y", "c")
DP_COL = ("z", "y", "c", "x")
MESH_ID = pl.DeviceIdType.MESH

RING = 4
RANK = 512
CHUNKS = 4
LANES = 128
TAG = 16
DIN_LOCAL = 2048
QUARTER = 256
TOKENS = 32768
TOP = 16000.0
SLOTS = (2, 1, 3)

INDEX_STEP = 747796405
MIX_ONE = 2127912213
MIX_TWO = 1103515245
HASH_ROWS = 64


PLAN = (
    ("partial_sketch", 0),
    ("partial_sketch", 1),
    ("sketch", 0),
    ("turn", 0),
    ("phase_one", 0),
    ("sketch", 1),
    ("phase_one", 1),
    ("relay", 0),
    ("sketch", 2),
    ("phase_one", 2),
    ("relay", 1),
    ("sketch", 3),
    ("phase_two", 0),
    ("phase_one", 3),
    ("relay", 2),
    ("phase_two", 1),
    ("phase_three", 0),
    ("relay", 3),
    ("phase_two", 2),
    ("phase_three", 1),
    ("phase_two", 3),
    ("phase_three", 2),
    ("phase_three", 3),
    ("finish", 0),
    ("finish", 1),
    ("finish", 2),
    ("finish", 3),
)


def wrapped(value):
    value &= 0xFFFFFFFF
    return value - (1 << 32) if value >= 1 << 31 else value


def ring(axis, step):
    return lax.rem(lax.axis_index(axis) + step, RING)


def coded(values):
    top = jnp.max(jnp.abs(values), axis=(0, 1), keepdims=True)
    exponent = jnp.floor(jnp.log2(jnp.maximum(top, 1e-30)))
    whole = jnp.round(values * (jnp.exp2(-exponent) * TOP)).astype(jnp.int16)
    tag = jnp.broadcast_to(exponent, (TAG, LANES)).astype(jnp.int16)
    return whole, tag


def decoded(ref, rows):
    exponent = ref[rows : rows + TAG, :].astype(jnp.float32)[0:1, :]
    return ref[0:rows, :].astype(jnp.float32) * (jnp.exp2(exponent) * (1.0 / TOP))


def store_coded(ref, rows, values):
    whole, tag = coded(values)
    ref[0:rows, :] = whole
    ref[rows : rows + TAG, :] = tag


def hash_signs(offset, first_row, part, out_ref):
    width = out_ref.shape[2]
    shape = (HASH_ROWS, width)
    base = lax.broadcasted_iota(jnp.int32, shape, 0) * wrapped(RANK * INDEX_STEP)
    base += (lax.broadcasted_iota(jnp.int32, shape, 1) + part * width) * INDEX_STEP

    def body(step, carry):
        row = pl.multiple_of(step * HASH_ROWS, HASH_ROWS)
        mixed = base + (offset + (first_row + row) * wrapped(RANK * INDEX_STEP))
        mixed = mixed ^ lax.shift_right_logical(mixed, jnp.int32(16))
        mixed = mixed * MIX_ONE
        mixed = mixed ^ lax.shift_right_logical(mixed, jnp.int32(13))
        mixed = mixed * wrapped(MIX_TWO << 11)
        out_ref[part, pl.ds(row, HASH_ROWS), :] = jnp.where(mixed < 0, -1.0, 1.0).astype(jnp.bfloat16)
        return carry

    lax.fori_loop(0, out_ref.shape[1] // HASH_ROWS, body, 0)


def reduce_kernel(
    seed_ref, step_ref, tokens_ref, grad_ref, momentum_ref,
    rows_ref, signs_ref,
    old, tok, sg, s_own, s_send, s_recv, sk, og, og_t,
    p_own, p_send, p_recv, q_own, q_send, q_recv, u_send, u_recv, t_send, t_recv,
    old_sem, tok_sem, og_sem, sg_sem, s_ss, s_rs, sk_ss, sk_rs,
    u_ss, u_rs, p_ss, p_rs, q_ss, q_rs, t_ss, t_rs,
):
    x, y, z, c = (lax.axis_index(name) for name in ("x", "y", "z", "c"))
    other = 1 - c
    first = (("y", "z"), ("z", "y"))

    barrier = pltpu.get_barrier_semaphore()
    for axis in ("x", "y", "z"):
        for step in SLOTS:
            pl.semaphore_signal(barrier, inc=1, device_id={axis: ring(axis, step)}, device_id_type=MESH_ID)
    pl.semaphore_signal(barrier, inc=1, device_id={"c": other}, device_id_type=MESH_ID)

    sems = {
        "s": (s_ss, s_rs), "k": (sk_ss, sk_rs), "u": (u_ss, u_rs), "p": (p_ss, p_rs), "q": (q_ss, q_rs), "t": (t_ss, t_rs)
    }
    sent = {}
    unsent = []

    def remote(src, dst, send_sem, recv_sem, where):
        return pltpu.make_async_remote_copy(
            src_ref=src, dst_ref=dst, send_sem=send_sem, recv_sem=recv_sem, device_id=where, device_id_type=MESH_ID
        )

    def send(kind, at, src, dst, where):
        out, into = sems[kind]
        copy = remote(src, dst, out.at[at], into.at[at], where)
        copy.start()
        sent[kind, at] = copy
        unsent.append((kind, at))

    def left(kind, at):
        sent[kind, at].wait_send()
        unsent.remove((kind, at))

    def arrived(kind, at, ref):
        pltpu.make_async_copy(ref, ref, sems[kind][1].at[at]).wait()

    tok_copies = {}
    for place, step in enumerate((2, 1, 3, 0)):
        at = pl.ds(pl.multiple_of(ring("x", step) * QUARTER, QUARTER), QUARTER)
        tok_copies[step] = pltpu.make_async_copy(tokens_ref.at[at], tok.at[at], tok_sem.at[place])
        tok_copies[step].start()
    mine = pl.ds(pl.multiple_of(c * QUARTER, QUARTER), QUARTER)
    theirs = pl.ds(pl.multiple_of(other * QUARTER, QUARTER), QUARTER)

    def columns(block, core):
        return pl.ds(pl.multiple_of((block * 2 + core) * 256, 256), 256)

    def start_own(block, carry):
        pltpu.make_async_copy(grad_ref.at[:, columns(block, c)], og.at[block, mine], og_sem.at[0]).start()
        return carry

    lax.fori_loop(0, 16, start_own, 0)
    old_copy = pltpu.make_async_copy(momentum_ref, old, old_sem)
    old_copy.start()

    offset = seed_ref[0] * 1664525 + step_ref[0] * 1013904223
    hash_signs(offset, x * DIN_LOCAL, 0, sg)

    pl.semaphore_wait(barrier, 10)

    def start_swap(block, carry):
        remote(grad_ref.at[:, columns(block, other)], og.at[block, mine], og_sem.at[1], og_sem.at[2], {"c": other}).start()
        return carry

    lax.fori_loop(0, 16, start_swap, 0)

    def partial_sketch(pair):
        def send_coded(k, step, values):
            slot = step - 1
            store_coded(s_send.at[k, slot], QUARTER, values)
            send("s", (k, slot), s_send.at[k, slot], s_recv.at[k, slot], {"x": ring("x", step)})

        if pair:
            hash_signs(offset, x * DIN_LOCAL, 1, sg)
            signs_out.start()
        for step in (2, 1, 3, 0):
            if not pair:
                tok_copies[step].wait()
            at = pl.ds(pl.multiple_of(ring("x", step) * QUARTER, QUARTER), QUARTER)
            part = jnp.dot(tok[at, :], sg[pair], preferred_element_type=jnp.float32)
            s_own[2 * pair + 1, step] = part[:, LANES:]
            if step:
                send_coded(2 * pair, step, part[:, :LANES])
            else:
                s_own[2 * pair, step] = part[:, :LANES]
        for step in SLOTS:
            send_coded(2 * pair + 1, step, s_own[2 * pair + 1, step])

    def turn(_):
        pltpu.make_async_copy(og.at[:, mine], og.at[:, mine], og_sem.at[0]).wait()
        swap.wait_recv()

        def body(block, carry):
            turned = og[block].T
            at_z = block // 4
            at_y = lax.rem(block, 4)
            for peer in range(RING):
                row = peer * 64
                og_t[0, at_y, pl.ds(pl.multiple_of(peer * 128 + at_z * 32, 32), 32), :] = turned[row : row + 32]
                og_t[1, at_z, pl.ds(pl.multiple_of(peer * 128 + at_y * 32, 32), 32), :] = turned[row + 32 : row + 64]
            return carry

        lax.fori_loop(0, 16, body, 0)

    def sketch(k):
        total = s_own[k, 0]
        for slot in range(3):
            arrived("s", (k, slot), s_recv.at[k, slot])
            total += decoded(s_recv.at[k, slot], QUARTER)
        sk[k, mine, :] = (total * (1.0 / jnp.sqrt(jnp.float32(RANK)))).astype(jnp.bfloat16)
        send("k", (k,), sk.at[k, mine], sk.at[k, mine], {"c": other})

    def phase_one(k):
        arrived("k", (k,), sk.at[k, theirs])
        right = sk[k]
        for step in (2, 1, 3, 0):
            for h, (axis, _) in enumerate(first):
                part = jnp.dot(og_t[h, ring(axis, step)], right, preferred_element_type=jnp.float32)
                if step == 2:
                    for side, near in enumerate((1, 3)):
                        ref = u_send.at[k, h, side]
                        store_coded(ref, 256, part[side * 256 : side * 256 + 256])
                        send("u", (k, h, side), ref, u_recv.at[k, h, side], {axis: ring(axis, near)})
                else:
                    p_own[k, h, (0, 1, None, 2)[step]] = part

    def relay(k):
        for side, near in enumerate((1, 3)):
            for h, (axis, _) in enumerate(first):
                arrived("u", (k, h, side), u_recv.at[k, h, side])
                rows_at = slice(side * 256, side * 256 + 256)
                p_own[k, h, side + 1, rows_at] += decoded(u_recv.at[k, h, side], 256)
                store_coded(p_send.at[k, h, side], 512, p_own[k, h, side + 1])
                send("p", (k, h, side), p_send.at[k, h, side], p_recv.at[k, h, side], {axis: ring(axis, near)})

    def phase_two(k):
        for h, (_, axis) in enumerate(first):
            total = p_own[k, h, 0]
            for side in range(2):
                arrived("p", (k, h, side), p_recv.at[k, h, side])
                total += decoded(p_recv.at[k, h, side], 512)
            p_own[k, h, 0] = total
            for step in (2, 1, 3, 0):
                at = [pl.ds(pl.multiple_of(peer * 128 + ring(axis, step) * 32, 32), 32) for peer in range(RING)]
                values = jnp.concatenate([p_own[k, h, 0, rows_at, :] for rows_at in at], axis=0)
                if step == 0:
                    q_own[k, h * 128 : h * 128 + 128] = values
                else:
                    slot = step - 1
                    store_coded(q_send.at[k, h, slot], 128, values)
                    send("q", (k, h, slot), q_send.at[k, h, slot], q_recv.at[k, h, slot], {axis: ring(axis, step)})

    def phase_three(k):
        if k == 0:
            old_copy.wait()
        for h in range(2):
            total = q_own[k, h * 128 : h * 128 + 128]
            for slot in range(3):
                arrived("q", (k, h, slot), q_recv.at[k, h, slot])
                total += decoded(q_recv.at[k, h, slot], 128)
            q_own[k, h * 128 : h * 128 + 128] = total * (0.2 / TOKENS)
            at = pl.ds(pl.multiple_of(h * 128 + x * 32, 32), 32)
            q_own[k, at, :] += 0.8 * old[h * 32 : h * 32 + 32, k * LANES : (k + 1) * LANES]
        store_coded(t_send.at[k], 256, q_own[k])
        for step in SLOTS:
            send("t", (k, step - 1), t_send.at[k], t_recv.at[k, step - 1], {"x": ring("x", step)})

    def finish(k):
        total = q_own[k]
        for step in SLOTS:
            arrived("t", (k, step - 1), t_recv.at[k, step - 1])
            total += decoded(t_recv.at[k, step - 1], 256)
        for peer in range(RING):
            for h in range(2):
                row = h * 128 + peer * 32
                rows_ref[k, peer * 64 + h * 32 : peer * 64 + h * 32 + 32, :] = total[row : row + 32]

    signs_out = pltpu.make_async_copy(sg, signs_ref, sg_sem)
    swap = remote(og.at[:, mine], og.at[:, theirs], og_sem.at[1], og_sem.at[2], {"c": other})
    steps = {
        "partial_sketch": partial_sketch, "turn": turn, "sketch": sketch, "phase_one": phase_one, "relay": relay,
        "phase_two": phase_two, "phase_three": phase_three, "finish": finish,
    }
    for name, k in PLAN:
        steps[name](k)
    swap.wait_send()
    signs_out.wait()
    for kind, at in tuple(unsent):
        left(kind, at)


def reduced(sign_seed, step_number, tokens, out_grad, momentum):
    f32, bf16, i16 = jnp.float32, jnp.bfloat16, jnp.int16
    dma = pltpu.SemaphoreType.DMA
    smem = pl.BlockSpec(memory_space=pltpu.SMEM)
    anywhere = pl.BlockSpec(memory_space=pltpu.HBM)
    vmem = pl.BlockSpec(memory_space=pltpu.VMEM)
    return pl.pallas_call(
        reduce_kernel,
        out_shape=(
            jax.ShapeDtypeStruct((CHUNKS, 256, LANES), f32),
            jax.ShapeDtypeStruct((2, DIN_LOCAL, 256), bf16),
        ),
        in_specs=[smem, smem, anywhere, anywhere, anywhere],
        out_specs=(vmem, anywhere),
        scratch_shapes=[
            pltpu.VMEM((64, RANK), f32),
            pltpu.VMEM((1024, DIN_LOCAL), bf16),
            pltpu.VMEM((2, DIN_LOCAL, 256), bf16),
            pltpu.VMEM((CHUNKS, RING, QUARTER, LANES), f32),
            pltpu.VMEM((CHUNKS, 3, QUARTER + TAG, LANES), i16),
            pltpu.VMEM((CHUNKS, 3, QUARTER + TAG, LANES), i16),
            pltpu.VMEM((CHUNKS, 512, LANES), bf16),
            pltpu.VMEM((16, 512, 256), bf16),
            pltpu.VMEM((2, RING, 512, 512), bf16),
            pltpu.VMEM((CHUNKS, 2, 3, 512, LANES), f32),
            pltpu.VMEM((CHUNKS, 2, 2, 512 + TAG, LANES), i16),
            pltpu.VMEM((CHUNKS, 2, 2, 512 + TAG, LANES), i16),
            pltpu.VMEM((CHUNKS, 256, LANES), f32),
            pltpu.VMEM((CHUNKS, 2, 3, 128 + TAG, LANES), i16),
            pltpu.VMEM((CHUNKS, 2, 3, 128 + TAG, LANES), i16),
            pltpu.VMEM((CHUNKS, 2, 2, 256 + TAG, LANES), i16),
            pltpu.VMEM((CHUNKS, 2, 2, 256 + TAG, LANES), i16),
            pltpu.VMEM((CHUNKS, 256 + TAG, LANES), i16),
            pltpu.VMEM((CHUNKS, 3, 256 + TAG, LANES), i16),
            dma, dma((4,)), dma((3,)), dma,
            dma((CHUNKS, 3)), dma((CHUNKS, 3)), dma((CHUNKS,)), dma((CHUNKS,)),
            dma((CHUNKS, 2, 2)), dma((CHUNKS, 2, 2)),
            dma((CHUNKS, 2, 2)), dma((CHUNKS, 2, 2)),
            dma((CHUNKS, 2, 3)), dma((CHUNKS, 2, 3)),
            dma((CHUNKS, 3)), dma((CHUNKS, 3)),
        ],
        compiler_params=pltpu.CompilerParams(
            collective_id=0, has_side_effects=True, vmem_limit_bytes=48 * 1024 * 1024
        ),
        name="sketch_and_reduce",
    )(sign_seed, step_number, tokens, out_grad, pltpu.with_memory_space_constraint(momentum, pltpu.HBM))


COLUMNS = 512


def update_kernel(
    rows_ref, signs_ref, weight_ref, second_ref, new_weight_ref, new_second_ref, momentum_ref,
    high, low, weight_out, second_out, weight_sem, second_sem,
):
    for k in range(CHUNKS):
        values = rows_ref[k]
        top = values.astype(jnp.bfloat16)
        high[:, k * LANES : (k + 1) * LANES] = top
        low[:, k * LANES : (k + 1) * LANES] = (values - top.astype(jnp.float32)).astype(jnp.bfloat16)
    copies = []
    for tile in range(DIN_LOCAL // COLUMNS):
        at = slice(tile * COLUMNS, (tile + 1) * COLUMNS)
        grad = jnp.zeros((256, COLUMNS), jnp.float32)
        for part in range(2):
            inner = slice(part * 256, (part + 1) * 256)
            for left in (high, low):
                grad += lax.dot_general(
                    left[:, inner], signs_ref[part, at, :], (((1,), (1,)), ((), ())), preferred_element_type=jnp.float32
                )
        grad = grad * (1.0 / jnp.sqrt(jnp.float32(RANK)))
        second = 0.95 * second_ref[:, at] + 0.05 * grad * grad
        second_out[tile] = second
        copies.append(pltpu.make_async_copy(second_out.at[tile], new_second_ref.at[:, at], second_sem.at[tile]))
        copies[-1].start()
        weight_out[tile] = weight_ref[:, at] - 0.5 * grad / (jnp.sqrt(second) + 1e-08)
        copies.append(pltpu.make_async_copy(weight_out.at[tile], new_weight_ref.at[:, at], weight_sem.at[tile]))
        copies[-1].start()
    mine = pl.ds(pl.multiple_of(lax.axis_index("x") * 64, 64), 64)
    for k in range(CHUNKS):
        momentum_ref[:, k * LANES : (k + 1) * LANES] = rows_ref[k, mine, :]
    for copy in copies:
        copy.wait()


def updated(rows, signs, weight, second):
    f32 = jnp.float32
    tiles = DIN_LOCAL // COLUMNS
    vmem = pl.BlockSpec(memory_space=pltpu.VMEM)
    hbm = pl.BlockSpec(memory_space=pltpu.HBM)
    return pl.pallas_call(
        update_kernel,
        out_shape=(
            jax.ShapeDtypeStruct(weight.shape, f32),
            jax.ShapeDtypeStruct(second.shape, f32),
            jax.ShapeDtypeStruct((64, RANK), f32),
        ),
        in_specs=[vmem, vmem, vmem, vmem],
        out_specs=(hbm, hbm, vmem),
        scratch_shapes=[
            pltpu.VMEM((256, RANK), jnp.bfloat16),
            pltpu.VMEM((256, RANK), jnp.bfloat16),
            pltpu.VMEM((tiles, 256, COLUMNS), f32),
            pltpu.VMEM((tiles, 256, COLUMNS), f32),
            pltpu.SemaphoreType.DMA((tiles,)),
            pltpu.SemaphoreType.DMA((tiles,)),
        ],
        compiler_params=pltpu.CompilerParams(vmem_limit_bytes=32 * 1024 * 1024),
        name="dense_update",
    )(rows, signs, weight, second)


def per_device(tokens, out_grad, weight, second, momentum, sign_seed, step_number):
    rows, signs = reduced(sign_seed, step_number, tokens, out_grad, momentum)
    return updated(rows, signs, weight, second)


def solution(mesh):
    torus = Mesh(mesh.devices.reshape(4, 4, 2, mesh.shape["col"]), ("z", "y", "c", "x"))
    return jax.shard_map(
        per_device,
        mesh=torus,
        in_specs=(
            P(DP, "x"),
            P(DP_COL, None),
            P(DP, "x"),
            P(DP, "x"),
            P(DP_COL, None),
            P(),
            P(),
        ),
        out_specs=(P(DP, "x"), P(DP, "x"), P(DP_COL, None)),
        check_vma=False,
    )
```

```python
import jax
import jax.numpy as jnp
from jax import lax
from jax.experimental import pallas as pl
from jax.experimental.pallas import tpu as pltpu
from jax.sharding import Mesh
from jax.sharding import PartitionSpec as P

DP = ("z", "y", "c")
DP_COL = ("z", "y", "c", "x")
MESH_ID = pl.DeviceIdType.MESH

RING = 4
RANK = 512
CHUNKS = 4
LANES = 128
TAG = 16
DIN_LOCAL = 2048
QUARTER = 256
TOKENS = 32768
TOP = 16000.0
SLOTS = (2, 1, 3)

INDEX_STEP = 747796405
MIX_ONE = 2127912213
MIX_TWO = 1103515245
HASH_ROWS = 64


PLAN = (
    ("partial_sketch", 0),
    ("partial_sketch", 1),
    ("sketch", 0),
    ("turn", 0),
    ("phase_one", 0),
    ("sketch", 1),
    ("phase_one", 1),
    ("relay", 0),
    ("sketch", 2),
    ("phase_one", 2),
    ("relay", 1),
    ("sketch", 3),
    ("phase_two", 0),
    ("phase_one", 3),
    ("relay", 2),
    ("phase_two", 1),
    ("phase_three", 0),
    ("relay", 3),
    ("phase_two", 2),
    ("phase_three", 1),
    ("phase_two", 3),
    ("phase_three", 2),
    ("phase_three", 3),
    ("finish", 0),
    ("finish", 1),
    ("dense", 0),
    ("finish", 2),
    ("dense", 1),
    ("finish", 3),
)


def wrapped(value):
    value &= 0xFFFFFFFF
    return value - (1 << 32) if value >= 1 << 31 else value


def ring(axis, step):
    return lax.rem(lax.axis_index(axis) + step, RING)


def coded(values):
    top = jnp.max(jnp.abs(values), axis=(0, 1), keepdims=True)
    exponent = jnp.floor(jnp.log2(jnp.maximum(top, 1e-30)))
    whole = jnp.round(values * (jnp.exp2(-exponent) * TOP)).astype(jnp.int16)
    tag = jnp.broadcast_to(exponent, (TAG, LANES)).astype(jnp.int16)
    return whole, tag


def decoded(ref, rows):
    exponent = ref[rows : rows + TAG, :].astype(jnp.float32)[0:1, :]
    return ref[0:rows, :].astype(jnp.float32) * (jnp.exp2(exponent) * (1.0 / TOP))


def store_coded(ref, rows, values):
    whole, tag = coded(values)
    ref[0:rows, :] = whole
    ref[rows : rows + TAG, :] = tag


def hash_signs(offset, first_row, part, out_ref):
    width = out_ref.shape[2]
    shape = (HASH_ROWS, width)
    base = lax.broadcasted_iota(jnp.int32, shape, 0) * wrapped(RANK * INDEX_STEP)
    base += (lax.broadcasted_iota(jnp.int32, shape, 1) + part * width) * INDEX_STEP

    def body(step, carry):
        row = pl.multiple_of(step * HASH_ROWS, HASH_ROWS)
        mixed = base + (offset + (first_row + row) * wrapped(RANK * INDEX_STEP))
        mixed = mixed ^ lax.shift_right_logical(mixed, jnp.int32(16))
        mixed = mixed * MIX_ONE
        mixed = mixed ^ lax.shift_right_logical(mixed, jnp.int32(13))
        mixed = mixed * wrapped(MIX_TWO << 11)
        out_ref[part, pl.ds(row, HASH_ROWS), :] = jnp.where(mixed < 0, -1.0, 1.0).astype(jnp.bfloat16)
        return carry

    lax.fori_loop(0, out_ref.shape[1] // HASH_ROWS, body, 0)


def halves(values):
    top = values.astype(jnp.bfloat16)
    return top, (values - top.astype(jnp.float32)).astype(jnp.bfloat16)


def times_signs(left, signs):
    return lax.dot_general(left, signs, (((1,), (1,)), ((), ())), preferred_element_type=jnp.float32)


def reduce_kernel(
    seed_ref, step_ref, tokens_ref, grad_ref, momentum_ref,
    rows_ref, signs_ref, dense_ref,
    old, tok, sg, s_own, s_send, s_recv, sk, og, og_t,
    p_own, p_send, p_recv, q_own, q_send, q_recv, u_send, u_recv, t_send, t_recv,
    old_sem, tok_sem, og_sem, sg_sem, s_ss, s_rs, sk_ss, sk_rs,
    u_ss, u_rs, p_ss, p_rs, q_ss, q_rs, t_ss, t_rs,
):
    x, y, z, c = (lax.axis_index(name) for name in ("x", "y", "z", "c"))
    other = 1 - c
    first = (("y", "z"), ("z", "y"))

    barrier = pltpu.get_barrier_semaphore()
    for axis in ("x", "y", "z"):
        for step in SLOTS:
            pl.semaphore_signal(barrier, inc=1, device_id={axis: ring(axis, step)}, device_id_type=MESH_ID)
    pl.semaphore_signal(barrier, inc=1, device_id={"c": other}, device_id_type=MESH_ID)

    sems = {
        "s": (s_ss, s_rs), "k": (sk_ss, sk_rs), "u": (u_ss, u_rs), "p": (p_ss, p_rs), "q": (q_ss, q_rs), "t": (t_ss, t_rs)
    }
    sent = {}
    unsent = []

    def remote(src, dst, send_sem, recv_sem, where):
        return pltpu.make_async_remote_copy(
            src_ref=src, dst_ref=dst, send_sem=send_sem, recv_sem=recv_sem, device_id=where, device_id_type=MESH_ID
        )

    def send(kind, at, src, dst, where):
        out, into = sems[kind]
        copy = remote(src, dst, out.at[at], into.at[at], where)
        copy.start()
        sent[kind, at] = copy
        unsent.append((kind, at))

    def left(kind, at):
        sent[kind, at].wait_send()
        unsent.remove((kind, at))

    def arrived(kind, at, ref):
        pltpu.make_async_copy(ref, ref, sems[kind][1].at[at]).wait()

    tok_copies = {}
    for place, step in enumerate((2, 1, 3, 0)):
        at = pl.ds(pl.multiple_of(ring("x", step) * QUARTER, QUARTER), QUARTER)
        tok_copies[step] = pltpu.make_async_copy(tokens_ref.at[at], tok.at[at], tok_sem.at[place])
        tok_copies[step].start()
    mine = pl.ds(pl.multiple_of(c * QUARTER, QUARTER), QUARTER)
    theirs = pl.ds(pl.multiple_of(other * QUARTER, QUARTER), QUARTER)

    def columns(block, core):
        return pl.ds(pl.multiple_of((block * 2 + core) * 256, 256), 256)

    def start_own(block, carry):
        pltpu.make_async_copy(grad_ref.at[:, columns(block, c)], og.at[block, mine], og_sem.at[0]).start()
        return carry

    lax.fori_loop(0, 16, start_own, 0)
    old_copy = pltpu.make_async_copy(momentum_ref, old, old_sem)
    old_copy.start()

    offset = seed_ref[0] * 1664525 + step_ref[0] * 1013904223
    hash_signs(offset, x * DIN_LOCAL, 0, sg)

    pl.semaphore_wait(barrier, 10)

    def start_swap(block, carry):
        remote(grad_ref.at[:, columns(block, other)], og.at[block, mine], og_sem.at[1], og_sem.at[2], {"c": other}).start()
        return carry

    lax.fori_loop(0, 16, start_swap, 0)

    def partial_sketch(pair):
        def send_coded(k, step, values):
            slot = step - 1
            store_coded(s_send.at[k, slot], QUARTER, values)
            send("s", (k, slot), s_send.at[k, slot], s_recv.at[k, slot], {"x": ring("x", step)})

        if pair:
            hash_signs(offset, x * DIN_LOCAL, 1, sg)
            signs_out.start()
        for step in (2, 1, 3, 0):
            if not pair:
                tok_copies[step].wait()
            at = pl.ds(pl.multiple_of(ring("x", step) * QUARTER, QUARTER), QUARTER)
            part = jnp.dot(tok[at, :], sg[pair], preferred_element_type=jnp.float32)
            s_own[2 * pair + 1, step] = part[:, LANES:]
            if step:
                send_coded(2 * pair, step, part[:, :LANES])
            else:
                s_own[2 * pair, step] = part[:, :LANES]
        for step in SLOTS:
            send_coded(2 * pair + 1, step, s_own[2 * pair + 1, step])

    def turn(_):
        pltpu.make_async_copy(og.at[:, mine], og.at[:, mine], og_sem.at[0]).wait()
        swap.wait_recv()

        def body(block, carry):
            turned = og[block].T
            at_z = block // 4
            at_y = lax.rem(block, 4)
            for peer in range(RING):
                row = peer * 64
                og_t[0, at_y, pl.ds(pl.multiple_of(peer * 128 + at_z * 32, 32), 32), :] = turned[row : row + 32]
                og_t[1, at_z, pl.ds(pl.multiple_of(peer * 128 + at_y * 32, 32), 32), :] = turned[row + 32 : row + 64]
            return carry

        lax.fori_loop(0, 16, body, 0)

    def sketch(k):
        total = s_own[k, 0]
        for slot in range(3):
            arrived("s", (k, slot), s_recv.at[k, slot])
            total += decoded(s_recv.at[k, slot], QUARTER)
        sk[k, mine, :] = (total * (1.0 / jnp.sqrt(jnp.float32(RANK)))).astype(jnp.bfloat16)
        send("k", (k,), sk.at[k, mine], sk.at[k, mine], {"c": other})

    def phase_one(k):
        arrived("k", (k,), sk.at[k, theirs])
        right = sk[k]
        for step in (2, 1, 3, 0):
            for h, (axis, _) in enumerate(first):
                part = jnp.dot(og_t[h, ring(axis, step)], right, preferred_element_type=jnp.float32)
                if step == 2:
                    for side, near in enumerate((1, 3)):
                        ref = u_send.at[k, h, side]
                        store_coded(ref, 256, part[side * 256 : side * 256 + 256])
                        send("u", (k, h, side), ref, u_recv.at[k, h, side], {axis: ring(axis, near)})
                else:
                    p_own[k, h, (0, 1, None, 2)[step]] = part

    def relay(k):
        for side, near in enumerate((1, 3)):
            for h, (axis, _) in enumerate(first):
                arrived("u", (k, h, side), u_recv.at[k, h, side])
                rows_at = slice(side * 256, side * 256 + 256)
                p_own[k, h, side + 1, rows_at] += decoded(u_recv.at[k, h, side], 256)
                store_coded(p_send.at[k, h, side], 512, p_own[k, h, side + 1])
                send("p", (k, h, side), p_send.at[k, h, side], p_recv.at[k, h, side], {axis: ring(axis, near)})

    def phase_two(k):
        for h, (_, axis) in enumerate(first):
            total = p_own[k, h, 0]
            for side in range(2):
                arrived("p", (k, h, side), p_recv.at[k, h, side])
                total += decoded(p_recv.at[k, h, side], 512)
            p_own[k, h, 0] = total
            for step in (2, 1, 3, 0):
                at = [pl.ds(pl.multiple_of(peer * 128 + ring(axis, step) * 32, 32), 32) for peer in range(RING)]
                values = jnp.concatenate([p_own[k, h, 0, rows_at, :] for rows_at in at], axis=0)
                if step == 0:
                    q_own[k, h * 128 : h * 128 + 128] = values
                else:
                    slot = step - 1
                    store_coded(q_send.at[k, h, slot], 128, values)
                    send("q", (k, h, slot), q_send.at[k, h, slot], q_recv.at[k, h, slot], {axis: ring(axis, step)})

    def phase_three(k):
        if k == 0:
            old_copy.wait()
        for h in range(2):
            total = q_own[k, h * 128 : h * 128 + 128]
            for slot in range(3):
                arrived("q", (k, h, slot), q_recv.at[k, h, slot])
                total += decoded(q_recv.at[k, h, slot], 128)
            q_own[k, h * 128 : h * 128 + 128] = total * (0.2 / TOKENS)
            at = pl.ds(pl.multiple_of(h * 128 + x * 32, 32), 32)
            q_own[k, at, :] += 0.8 * old[h * 32 : h * 32 + 32, k * LANES : (k + 1) * LANES]
        store_coded(t_send.at[k], 256, q_own[k])
        for step in SLOTS:
            send("t", (k, step - 1), t_send.at[k], t_recv.at[k, step - 1], {"x": ring("x", step)})

    def finish(k):
        total = q_own[k]
        for step in SLOTS:
            arrived("t", (k, step - 1), t_recv.at[k, step - 1])
            total += decoded(t_recv.at[k, step - 1], 256)
        for peer in range(RING):
            for h in range(2):
                row = h * 128 + peer * 32
                rows_ref[k, peer * 64 + h * 32 : peer * 64 + h * 32 + 32, :] = total[row : row + 32]

    def dense(part):
        chunks = ((0, 1), (2,))[part]
        inner = slice(0, len(chunks) * LANES)
        pairs = [halves(rows_ref[k]) for k in chunks]
        top = jnp.concatenate([pair[0] for pair in pairs], axis=1)
        rest = jnp.concatenate([pair[1] for pair in pairs], axis=1)

        def body(tile, carry):
            at = pl.ds(pl.multiple_of(tile * 512, 512), 512)
            grad = times_signs(top, sg[part, at, inner]) + times_signs(rest, sg[part, at, inner])
            if part:
                grad += dense_ref[tile]
            dense_ref[tile] = grad
            return carry

        lax.fori_loop(0, DIN_LOCAL // 512, body, 0)

    signs_out = pltpu.make_async_copy(sg.at[1, :, LANES:], signs_ref, sg_sem)
    swap = remote(og.at[:, mine], og.at[:, theirs], og_sem.at[1], og_sem.at[2], {"c": other})
    steps = {
        "partial_sketch": partial_sketch, "turn": turn, "sketch": sketch, "phase_one": phase_one, "relay": relay,
        "phase_two": phase_two, "phase_three": phase_three, "finish": finish, "dense": dense,
    }
    for name, k in PLAN:
        steps[name](k)
    swap.wait_send()
    signs_out.wait()
    for kind, at in tuple(unsent):
        left(kind, at)


def reduced(sign_seed, step_number, tokens, out_grad, momentum):
    f32, bf16, i16 = jnp.float32, jnp.bfloat16, jnp.int16
    dma = pltpu.SemaphoreType.DMA
    smem = pl.BlockSpec(memory_space=pltpu.SMEM)
    anywhere = pl.BlockSpec(memory_space=pltpu.HBM)
    vmem = pl.BlockSpec(memory_space=pltpu.VMEM)
    return pl.pallas_call(
        reduce_kernel,
        out_shape=(
            jax.ShapeDtypeStruct((CHUNKS, 256, LANES), f32),
            jax.ShapeDtypeStruct((DIN_LOCAL, LANES), bf16),
            jax.ShapeDtypeStruct((DIN_LOCAL // 512, 256, 512), f32),
        ),
        in_specs=[smem, smem, anywhere, anywhere, anywhere],
        out_specs=(vmem, anywhere, vmem),
        scratch_shapes=[
            pltpu.VMEM((64, RANK), f32),
            pltpu.VMEM((1024, DIN_LOCAL), bf16),
            pltpu.VMEM((2, DIN_LOCAL, 256), bf16),
            pltpu.VMEM((CHUNKS, RING, QUARTER, LANES), f32),
            pltpu.VMEM((CHUNKS, 3, QUARTER + TAG, LANES), i16),
            pltpu.VMEM((CHUNKS, 3, QUARTER + TAG, LANES), i16),
            pltpu.VMEM((CHUNKS, 512, LANES), bf16),
            pltpu.VMEM((16, 512, 256), bf16),
            pltpu.VMEM((2, RING, 512, 512), bf16),
            pltpu.VMEM((CHUNKS, 2, 3, 512, LANES), f32),
            pltpu.VMEM((CHUNKS, 2, 2, 512 + TAG, LANES), i16),
            pltpu.VMEM((CHUNKS, 2, 2, 512 + TAG, LANES), i16),
            pltpu.VMEM((CHUNKS, 256, LANES), f32),
            pltpu.VMEM((CHUNKS, 2, 3, 128 + TAG, LANES), i16),
            pltpu.VMEM((CHUNKS, 2, 3, 128 + TAG, LANES), i16),
            pltpu.VMEM((CHUNKS, 2, 2, 256 + TAG, LANES), i16),
            pltpu.VMEM((CHUNKS, 2, 2, 256 + TAG, LANES), i16),
            pltpu.VMEM((CHUNKS, 256 + TAG, LANES), i16),
            pltpu.VMEM((CHUNKS, 3, 256 + TAG, LANES), i16),
            dma, dma((4,)), dma((3,)), dma,
            dma((CHUNKS, 3)), dma((CHUNKS, 3)), dma((CHUNKS,)), dma((CHUNKS,)),
            dma((CHUNKS, 2, 2)), dma((CHUNKS, 2, 2)),
            dma((CHUNKS, 2, 2)), dma((CHUNKS, 2, 2)),
            dma((CHUNKS, 2, 3)), dma((CHUNKS, 2, 3)),
            dma((CHUNKS, 3)), dma((CHUNKS, 3)),
        ],
        compiler_params=pltpu.CompilerParams(
            collective_id=0, has_side_effects=True, vmem_limit_bytes=48 * 1024 * 1024
        ),
        name="sketch_and_reduce",
    )(sign_seed, step_number, tokens, out_grad, pltpu.with_memory_space_constraint(momentum, pltpu.HBM))


COLUMNS = 512


def update_kernel(
    rows_ref, signs_ref, dense_ref, weight_ref, second_ref, new_weight_ref, new_second_ref, momentum_ref,
    weight_out, second_out, weight_sem, second_sem,
):
    top, rest = halves(rows_ref[CHUNKS - 1])
    copies = []
    for tile in range(DIN_LOCAL // COLUMNS):
        at = slice(tile * COLUMNS, (tile + 1) * COLUMNS)
        grad = dense_ref[tile] + times_signs(top, signs_ref[at, :]) + times_signs(rest, signs_ref[at, :])
        grad = grad * (1.0 / jnp.sqrt(jnp.float32(RANK)))
        second = 0.95 * second_ref[:, at] + 0.05 * grad * grad
        second_out[tile] = second
        copies.append(pltpu.make_async_copy(second_out.at[tile], new_second_ref.at[:, at], second_sem.at[tile]))
        copies[-1].start()
        weight_out[tile] = weight_ref[:, at] - 0.5 * grad / (jnp.sqrt(second) + 1e-08)
        copies.append(pltpu.make_async_copy(weight_out.at[tile], new_weight_ref.at[:, at], weight_sem.at[tile]))
        copies[-1].start()
    mine = pl.ds(pl.multiple_of(lax.axis_index("x") * 64, 64), 64)
    for k in range(CHUNKS):
        momentum_ref[:, k * LANES : (k + 1) * LANES] = rows_ref[k, mine, :]
    for copy in copies:
        copy.wait()


def updated(rows, signs, dense, weight, second):
    f32 = jnp.float32
    tiles = DIN_LOCAL // COLUMNS
    vmem = pl.BlockSpec(memory_space=pltpu.VMEM)
    hbm = pl.BlockSpec(memory_space=pltpu.HBM)
    return pl.pallas_call(
        update_kernel,
        out_shape=(
            jax.ShapeDtypeStruct(weight.shape, f32),
            jax.ShapeDtypeStruct(second.shape, f32),
            jax.ShapeDtypeStruct((64, RANK), f32),
        ),
        in_specs=[vmem, vmem, vmem, vmem, vmem],
        out_specs=(hbm, hbm, vmem),
        scratch_shapes=[
            pltpu.VMEM((tiles, 256, COLUMNS), f32),
            pltpu.VMEM((tiles, 256, COLUMNS), f32),
            pltpu.SemaphoreType.DMA((tiles,)),
            pltpu.SemaphoreType.DMA((tiles,)),
        ],
        compiler_params=pltpu.CompilerParams(vmem_limit_bytes=32 * 1024 * 1024),
        name="dense_update",
    )(rows, signs, dense, weight, second)


def per_device(tokens, out_grad, weight, second, momentum, sign_seed, step_number):
    rows, signs, dense = reduced(sign_seed, step_number, tokens, out_grad, momentum)
    return updated(rows, signs, dense, weight, second)


def solution(mesh):
    torus = Mesh(mesh.devices.reshape(4, 4, 2, mesh.shape["col"]), ("z", "y", "c", "x"))
    return jax.shard_map(
        per_device,
        mesh=torus,
        in_specs=(
            P(DP, "x"),
            P(DP_COL, None),
            P(DP, "x"),
            P(DP, "x"),
            P(DP_COL, None),
            P(),
            P(),
        ),
        out_specs=(P(DP, "x"), P(DP, "x"), P(DP_COL, None)),
        check_vma=False,
    )
```

```python
import jax
import jax.numpy as jnp
from jax import lax
from jax.experimental import pallas as pl
from jax.experimental.pallas import tpu as pltpu
from jax.sharding import Mesh
from jax.sharding import PartitionSpec as P

DP = ("z", "y", "c")
DP_COL = ("z", "y", "c", "x")
MESH_ID = pl.DeviceIdType.MESH

RING = 4
RANK = 512
CHUNKS = 4
LANES = 128
TAG = 8
DIN_LOCAL = 2048
QUARTER = 256
TOKENS = 32768
TOP = 16000.0
SLOTS = (2, 1, 3)

INDEX_STEP = 747796405
MIX_ONE = 2127912213
MIX_TWO = 1103515245
HASH_ROWS = 64


PLAN = (
    ("partial_sketch", 0),
    ("partial_sketch", 1),
    ("sketch", 0),
    ("turn", 0),
    ("phase_one", 0),
    ("sketch", 1),
    ("phase_one", 1),
    ("relay", 0),
    ("sketch", 2),
    ("phase_one", 2),
    ("relay", 1),
    ("sketch", 3),
    ("phase_two", 0),
    ("phase_one", 3),
    ("relay", 2),
    ("phase_two", 1),
    ("phase_three", 0),
    ("relay", 3),
    ("phase_two", 2),
    ("phase_three", 1),
    ("phase_two", 3),
    ("phase_three", 2),
    ("phase_three", 3),
    ("finish", 0),
    ("finish", 1),
    ("dense", 0),
    ("finish", 2),
    ("dense", 1),
    ("finish", 3),
)


def wrapped(value):
    value &= 0xFFFFFFFF
    return value - (1 << 32) if value >= 1 << 31 else value


def ring(axis, step):
    return lax.rem(lax.axis_index(axis) + step, RING)


def coded(values):
    top = jnp.max(jnp.abs(values), axis=(0, 1), keepdims=True)
    exponent = jnp.floor(jnp.log2(jnp.maximum(top, 1e-30)))
    whole = jnp.round(values * (jnp.exp2(-exponent) * TOP)).astype(jnp.int16)
    tag = jnp.broadcast_to(exponent, (TAG, LANES)).astype(jnp.int16)
    return whole, tag


def decoded(ref, rows):
    exponent = ref[rows : rows + TAG, :].astype(jnp.float32)[0:1, :]
    return ref[0:rows, :].astype(jnp.float32) * (jnp.exp2(exponent) * (1.0 / TOP))


def store_coded(ref, rows, values):
    whole, tag = coded(values)
    ref[0:rows, :] = whole
    ref[rows : rows + TAG, :] = tag


def hash_signs(offset, first_row, part, out_ref):
    width = out_ref.shape[2]
    shape = (HASH_ROWS, width)
    base = lax.broadcasted_iota(jnp.int32, shape, 0) * wrapped(RANK * INDEX_STEP)
    base += (lax.broadcasted_iota(jnp.int32, shape, 1) + part * width) * INDEX_STEP

    def body(step, carry):
        row = pl.multiple_of(step * HASH_ROWS, HASH_ROWS)
        mixed = base + (offset + (first_row + row) * wrapped(RANK * INDEX_STEP))
        mixed = mixed ^ lax.shift_right_logical(mixed, jnp.int32(16))
        mixed = mixed * MIX_ONE
        mixed = mixed ^ lax.shift_right_logical(mixed, jnp.int32(13))
        mixed = mixed * wrapped(MIX_TWO << 11)
        out_ref[part, pl.ds(row, HASH_ROWS), :] = jnp.where(mixed < 0, -1.0, 1.0).astype(jnp.bfloat16)
        return carry

    lax.fori_loop(0, out_ref.shape[1] // HASH_ROWS, body, 0)


def halves(values):
    top = values.astype(jnp.bfloat16)
    return top, (values - top.astype(jnp.float32)).astype(jnp.bfloat16)


def times_signs(left, signs):
    return lax.dot_general(left, signs, (((1,), (1,)), ((), ())), preferred_element_type=jnp.float32)


def reduce_kernel(
    seed_ref, step_ref, tokens_ref, grad_ref, momentum_ref,
    rows_ref, signs_ref, dense_ref,
    old, tok, sg, s_own, s_send, s_recv, sk, og, og_t,
    p_own, p_send, p_recv, q_own, q_send, q_recv, u_send, u_recv, t_send, t_recv,
    old_sem, tok_sem, og_sem, sg_sem, s_ss, s_rs, sk_ss, sk_rs,
    u_ss, u_rs, p_ss, p_rs, q_ss, q_rs, t_ss, t_rs,
):
    x, y, z, c = (lax.axis_index(name) for name in ("x", "y", "z", "c"))
    other = 1 - c
    first = (("y", "z"), ("z", "y"))

    barrier = pltpu.get_barrier_semaphore()
    for axis in ("x", "y", "z"):
        for step in SLOTS:
            pl.semaphore_signal(barrier, inc=1, device_id={axis: ring(axis, step)}, device_id_type=MESH_ID)
    pl.semaphore_signal(barrier, inc=1, device_id={"c": other}, device_id_type=MESH_ID)

    sems = {
        "s": (s_ss, s_rs), "k": (sk_ss, sk_rs), "u": (u_ss, u_rs), "p": (p_ss, p_rs), "q": (q_ss, q_rs), "t": (t_ss, t_rs)
    }
    sent = {}
    unsent = []

    def remote(src, dst, send_sem, recv_sem, where):
        return pltpu.make_async_remote_copy(
            src_ref=src, dst_ref=dst, send_sem=send_sem, recv_sem=recv_sem, device_id=where, device_id_type=MESH_ID
        )

    def send(kind, at, src, dst, where):
        out, into = sems[kind]
        copy = remote(src, dst, out.at[at], into.at[at], where)
        copy.start()
        sent[kind, at] = copy
        unsent.append((kind, at))

    def left(kind, at):
        sent[kind, at].wait_send()
        unsent.remove((kind, at))

    def arrived(kind, at, ref):
        pltpu.make_async_copy(ref, ref, sems[kind][1].at[at]).wait()

    tok_copies = {}
    for place, step in enumerate((2, 1, 3, 0)):
        at = pl.ds(pl.multiple_of(ring("x", step) * QUARTER, QUARTER), QUARTER)
        tok_copies[step] = pltpu.make_async_copy(tokens_ref.at[at], tok.at[at], tok_sem.at[place])
        tok_copies[step].start()
    mine = pl.ds(pl.multiple_of(c * QUARTER, QUARTER), QUARTER)
    theirs = pl.ds(pl.multiple_of(other * QUARTER, QUARTER), QUARTER)

    def columns(block, core):
        return pl.ds(pl.multiple_of((block * 2 + core) * 256, 256), 256)

    def start_own(block, carry):
        pltpu.make_async_copy(grad_ref.at[:, columns(block, c)], og.at[block, mine], og_sem.at[0]).start()
        return carry

    lax.fori_loop(0, 16, start_own, 0)
    old_copy = pltpu.make_async_copy(momentum_ref, old, old_sem)
    old_copy.start()

    offset = seed_ref[0] * 1664525 + step_ref[0] * 1013904223
    hash_signs(offset, x * DIN_LOCAL, 0, sg)

    pl.semaphore_wait(barrier, 10)

    def start_swap(block, carry):
        remote(grad_ref.at[:, columns(block, other)], og.at[block, mine], og_sem.at[1], og_sem.at[2], {"c": other}).start()
        return carry

    lax.fori_loop(0, 16, start_swap, 0)

    def partial_sketch(pair):
        def send_coded(k, step, values):
            slot = step - 1
            store_coded(s_send.at[k, slot], QUARTER, values)
            send("s", (k, slot), s_send.at[k, slot], s_recv.at[k, slot], {"x": ring("x", step)})

        if pair:
            hash_signs(offset, x * DIN_LOCAL, 1, sg)
            signs_out.start()
        for step in (2, 1, 3, 0):
            if not pair:
                tok_copies[step].wait()
            at = pl.ds(pl.multiple_of(ring("x", step) * QUARTER, QUARTER), QUARTER)
            part = jnp.dot(tok[at, :], sg[pair], preferred_element_type=jnp.float32)
            s_own[2 * pair + 1, step] = part[:, LANES:]
            if step:
                send_coded(2 * pair, step, part[:, :LANES])
            else:
                s_own[2 * pair, step] = part[:, :LANES]
        for step in SLOTS:
            send_coded(2 * pair + 1, step, s_own[2 * pair + 1, step])

    def turn(_):
        pltpu.make_async_copy(og.at[:, mine], og.at[:, mine], og_sem.at[0]).wait()
        swap.wait_recv()

        def body(block, carry):
            turned = og[block].T
            at_z = block // 4
            at_y = lax.rem(block, 4)
            for peer in range(RING):
                row = peer * 64
                og_t[0, at_y, pl.ds(pl.multiple_of(peer * 128 + at_z * 32, 32), 32), :] = turned[row : row + 32]
                og_t[1, at_z, pl.ds(pl.multiple_of(peer * 128 + at_y * 32, 32), 32), :] = turned[row + 32 : row + 64]
            return carry

        lax.fori_loop(0, 16, body, 0)

    def sketch(k):
        total = s_own[k, 0]
        for slot in range(3):
            arrived("s", (k, slot), s_recv.at[k, slot])
            total += decoded(s_recv.at[k, slot], QUARTER)
        sk[k, mine, :] = (total * (1.0 / jnp.sqrt(jnp.float32(RANK)))).astype(jnp.bfloat16)
        send("k", (k,), sk.at[k, mine], sk.at[k, mine], {"c": other})

    def phase_one(k):
        arrived("k", (k,), sk.at[k, theirs])
        right = sk[k]
        for step in (2, 1, 3, 0):
            for h, (axis, _) in enumerate(first):
                part = jnp.dot(og_t[h, ring(axis, step)], right, preferred_element_type=jnp.float32)
                if step == 2:
                    for side, near in enumerate((1, 3)):
                        ref = u_send.at[k, h, side]
                        store_coded(ref, 256, part[side * 256 : side * 256 + 256])
                        send("u", (k, h, side), ref, u_recv.at[k, h, side], {axis: ring(axis, near)})
                else:
                    p_own[k, h, (0, 1, None, 2)[step]] = part

    def relay(k):
        for side, near in enumerate((1, 3)):
            for h, (axis, _) in enumerate(first):
                arrived("u", (k, h, side), u_recv.at[k, h, side])
                rows_at = slice(side * 256, side * 256 + 256)
                p_own[k, h, side + 1, rows_at] += decoded(u_recv.at[k, h, side], 256)
                store_coded(p_send.at[k, h, side], 512, p_own[k, h, side + 1])
                send("p", (k, h, side), p_send.at[k, h, side], p_recv.at[k, h, side], {axis: ring(axis, near)})

    def phase_two(k):
        for h, (_, axis) in enumerate(first):
            total = p_own[k, h, 0]
            for side in range(2):
                arrived("p", (k, h, side), p_recv.at[k, h, side])
                total += decoded(p_recv.at[k, h, side], 512)
            p_own[k, h, 0] = total
            for step in (2, 1, 3, 0):
                at = [pl.ds(pl.multiple_of(peer * 128 + ring(axis, step) * 32, 32), 32) for peer in range(RING)]
                values = jnp.concatenate([p_own[k, h, 0, rows_at, :] for rows_at in at], axis=0)
                if step == 0:
                    q_own[k, h * 128 : h * 128 + 128] = values
                else:
                    slot = step - 1
                    store_coded(q_send.at[k, h, slot], 128, values)
                    send("q", (k, h, slot), q_send.at[k, h, slot], q_recv.at[k, h, slot], {axis: ring(axis, step)})

    def phase_three(k):
        if k == 0:
            old_copy.wait()
        for h in range(2):
            total = q_own[k, h * 128 : h * 128 + 128]
            for slot in range(3):
                arrived("q", (k, h, slot), q_recv.at[k, h, slot])
                total += decoded(q_recv.at[k, h, slot], 128)
            q_own[k, h * 128 : h * 128 + 128] = total * (0.2 / TOKENS)
            at = pl.ds(pl.multiple_of(h * 128 + x * 32, 32), 32)
            q_own[k, at, :] += 0.8 * old[h * 32 : h * 32 + 32, k * LANES : (k + 1) * LANES]
        store_coded(t_send.at[k], 256, q_own[k])
        for step in SLOTS:
            send("t", (k, step - 1), t_send.at[k], t_recv.at[k, step - 1], {"x": ring("x", step)})

    def finish(k):
        total = q_own[k]
        for step in SLOTS:
            arrived("t", (k, step - 1), t_recv.at[k, step - 1])
            total += decoded(t_recv.at[k, step - 1], 256)
        for peer in range(RING):
            for h in range(2):
                row = h * 128 + peer * 32
                rows_ref[k, peer * 64 + h * 32 : peer * 64 + h * 32 + 32, :] = total[row : row + 32]

    def dense(part):
        chunks = ((0, 1), (2,))[part]
        inner = slice(0, len(chunks) * LANES)
        pairs = [halves(rows_ref[k]) for k in chunks]
        top = jnp.concatenate([pair[0] for pair in pairs], axis=1)
        rest = jnp.concatenate([pair[1] for pair in pairs], axis=1)

        def body(tile, carry):
            at = pl.ds(pl.multiple_of(tile * 512, 512), 512)
            grad = times_signs(top, sg[part, at, inner]) + times_signs(rest, sg[part, at, inner])
            if part:
                grad += dense_ref[tile]
            dense_ref[tile] = grad
            return carry

        lax.fori_loop(0, DIN_LOCAL // 512, body, 0)

    signs_out = pltpu.make_async_copy(sg.at[1, :, LANES:], signs_ref, sg_sem)
    swap = remote(og.at[:, mine], og.at[:, theirs], og_sem.at[1], og_sem.at[2], {"c": other})
    steps = {
        "partial_sketch": partial_sketch, "turn": turn, "sketch": sketch, "phase_one": phase_one, "relay": relay,
        "phase_two": phase_two, "phase_three": phase_three, "finish": finish, "dense": dense,
    }
    for name, k in PLAN:
        steps[name](k)
    swap.wait_send()
    signs_out.wait()
    for kind, at in tuple(unsent):
        left(kind, at)


def reduced(sign_seed, step_number, tokens, out_grad, momentum):
    f32, bf16, i16 = jnp.float32, jnp.bfloat16, jnp.int16
    dma = pltpu.SemaphoreType.DMA
    smem = pl.BlockSpec(memory_space=pltpu.SMEM)
    anywhere = pl.BlockSpec(memory_space=pltpu.HBM)
    vmem = pl.BlockSpec(memory_space=pltpu.VMEM)
    return pl.pallas_call(
        reduce_kernel,
        out_shape=(
            jax.ShapeDtypeStruct((CHUNKS, 256, LANES), f32),
            jax.ShapeDtypeStruct((DIN_LOCAL, LANES), bf16),
            jax.ShapeDtypeStruct((DIN_LOCAL // 512, 256, 512), f32),
        ),
        in_specs=[smem, smem, anywhere, anywhere, anywhere],
        out_specs=(vmem, anywhere, vmem),
        scratch_shapes=[
            pltpu.VMEM((64, RANK), f32),
            pltpu.VMEM((1024, DIN_LOCAL), bf16),
            pltpu.VMEM((2, DIN_LOCAL, 256), bf16),
            pltpu.VMEM((CHUNKS, RING, QUARTER, LANES), f32),
            pltpu.VMEM((CHUNKS, 3, QUARTER + TAG, LANES), i16),
            pltpu.VMEM((CHUNKS, 3, QUARTER + TAG, LANES), i16),
            pltpu.VMEM((CHUNKS, 512, LANES), bf16),
            pltpu.VMEM((16, 512, 256), bf16),
            pltpu.VMEM((2, RING, 512, 512), bf16),
            pltpu.VMEM((CHUNKS, 2, 3, 512, LANES), f32),
            pltpu.VMEM((CHUNKS, 2, 2, 512 + TAG, LANES), i16),
            pltpu.VMEM((CHUNKS, 2, 2, 512 + TAG, LANES), i16),
            pltpu.VMEM((CHUNKS, 256, LANES), f32),
            pltpu.VMEM((CHUNKS, 2, 3, 128 + TAG, LANES), i16),
            pltpu.VMEM((CHUNKS, 2, 3, 128 + TAG, LANES), i16),
            pltpu.VMEM((CHUNKS, 2, 2, 256 + TAG, LANES), i16),
            pltpu.VMEM((CHUNKS, 2, 2, 256 + TAG, LANES), i16),
            pltpu.VMEM((CHUNKS, 256 + TAG, LANES), i16),
            pltpu.VMEM((CHUNKS, 3, 256 + TAG, LANES), i16),
            dma, dma((4,)), dma((3,)), dma,
            dma((CHUNKS, 3)), dma((CHUNKS, 3)), dma((CHUNKS,)), dma((CHUNKS,)),
            dma((CHUNKS, 2, 2)), dma((CHUNKS, 2, 2)),
            dma((CHUNKS, 2, 2)), dma((CHUNKS, 2, 2)),
            dma((CHUNKS, 2, 3)), dma((CHUNKS, 2, 3)),
            dma((CHUNKS, 3)), dma((CHUNKS, 3)),
        ],
        compiler_params=pltpu.CompilerParams(
            collective_id=0, has_side_effects=True, vmem_limit_bytes=48 * 1024 * 1024
        ),
        name="sketch_and_reduce",
    )(sign_seed, step_number, tokens, out_grad, pltpu.with_memory_space_constraint(momentum, pltpu.HBM))


COLUMNS = 512


def update_kernel(
    rows_ref, signs_ref, dense_ref, weight_ref, second_ref, new_weight_ref, new_second_ref, momentum_ref,
    weight_out, second_out, weight_sem, second_sem,
):
    top, rest = halves(rows_ref[CHUNKS - 1])
    copies = []
    for tile in range(DIN_LOCAL // COLUMNS):
        at = slice(tile * COLUMNS, (tile + 1) * COLUMNS)
        grad = dense_ref[tile] + times_signs(top, signs_ref[at, :]) + times_signs(rest, signs_ref[at, :])
        grad = grad * (1.0 / jnp.sqrt(jnp.float32(RANK)))
        second = 0.95 * second_ref[:, at] + 0.05 * grad * grad
        second_out[tile] = second
        copies.append(pltpu.make_async_copy(second_out.at[tile], new_second_ref.at[:, at], second_sem.at[tile]))
        copies[-1].start()
        weight_out[tile] = weight_ref[:, at] - 0.5 * grad / (jnp.sqrt(second) + 1e-08)
        copies.append(pltpu.make_async_copy(weight_out.at[tile], new_weight_ref.at[:, at], weight_sem.at[tile]))
        copies[-1].start()
    mine = pl.ds(pl.multiple_of(lax.axis_index("x") * 64, 64), 64)
    for k in range(CHUNKS):
        momentum_ref[:, k * LANES : (k + 1) * LANES] = rows_ref[k, mine, :]
    for copy in copies:
        copy.wait()


def updated(rows, signs, dense, weight, second):
    f32 = jnp.float32
    tiles = DIN_LOCAL // COLUMNS
    vmem = pl.BlockSpec(memory_space=pltpu.VMEM)
    hbm = pl.BlockSpec(memory_space=pltpu.HBM)
    return pl.pallas_call(
        update_kernel,
        out_shape=(
            jax.ShapeDtypeStruct(weight.shape, f32),
            jax.ShapeDtypeStruct(second.shape, f32),
            jax.ShapeDtypeStruct((64, RANK), f32),
        ),
        in_specs=[vmem, vmem, vmem, vmem, vmem],
        out_specs=(hbm, hbm, vmem),
        scratch_shapes=[
            pltpu.VMEM((tiles, 256, COLUMNS), f32),
            pltpu.VMEM((tiles, 256, COLUMNS), f32),
            pltpu.SemaphoreType.DMA((tiles,)),
            pltpu.SemaphoreType.DMA((tiles,)),
        ],
        compiler_params=pltpu.CompilerParams(vmem_limit_bytes=32 * 1024 * 1024),
        name="dense_update",
    )(rows, signs, dense, weight, second)


def per_device(tokens, out_grad, weight, second, momentum, sign_seed, step_number):
    rows, signs, dense = reduced(sign_seed, step_number, tokens, out_grad, momentum)
    return updated(rows, signs, dense, weight, second)


def solution(mesh):
    torus = Mesh(mesh.devices.reshape(4, 4, 2, mesh.shape["col"]), ("z", "y", "c", "x"))
    return jax.shard_map(
        per_device,
        mesh=torus,
        in_specs=(
            P(DP, "x"),
            P(DP_COL, None),
            P(DP, "x"),
            P(DP, "x"),
            P(DP_COL, None),
            P(),
            P(),
        ),
        out_specs=(P(DP, "x"), P(DP, "x"), P(DP_COL, None)),
        check_vma=False,
    )
```
